256 devices in a mesh: pair: 2 (over core), virt: 4 (over x), integ: 32 (over y, z).
Axes of the slice: x: 4, y: 4, z: 8, core: 2. Of those that a mesh axis runs over, the one named last changes fastest.
Arguments:
- amplitudes: bfloat16 [2, 32, 256, 256], P('pair', 'integ', 'virt'), may hold values from -4 to 4
- vv_factors: bfloat16 [512, 256, 256], P('integ'), may hold values from -0.25 to 0.25
- ov_factors: bfloat16 [512, 32, 256], P(None, 'integ'), may hold values from -0.75 to 0.75
- occ_energy_i: float32 [2], P('pair'), may hold values from -2 to -0.5
- occ_energy_j: float32 [32], P('integ'), may hold values from -2 to -0.5
- virt_energy: float32 [256], replicated, may hold values from 0.2 to 3
- vv_mask: int32 [2, 2], replicated, may hold values 0 or 1
- pair_domain: int32 [2, 32, 2], P('pair', 'integ'), may hold values 0 or 1
Outputs:
- update: bfloat16 [2, 32, 256, 256], P('pair', 'integ', 'virt')
The draws below stay inside these ranges and needn't reach their ends.
All inputs are finite; a program needn't handle non-finite values. No bound on the sum of `pair_domain` on one device may be relied on, other than what follows from the above.
Results may differ from the reference program's by a relative error of at most 0.014.
Values may be sent and summed in bfloat16 or wider, within the bound.
No kernel may reach another device: no remote copies, remote signals or barrier semaphores. Data moves between devices by JAX's collectives and lax.ppermute only.
A program may use at most 64 MiB of HBM per device.

```python
import jax
import jax.numpy as jnp
from jax import lax

TILE_SIZE = 128
TILES = 2
AUX_DEV = 16
VIRTUALS = 256
AUXILIARY = 512
OCC_OWNED = 2
OCC_SLAB = 32


def plant(result, own_key, smallest, largest):
    place = [jax.random.randint(jax.random.fold_in(own_key, axis), (), 0, length) for axis, length in enumerate(result.shape)]
    widest = result.shape.index(max(result.shape))
    beside = place[:widest] + [(place[widest] + 1) % result.shape[widest]] + place[widest + 1:]
    return result.at[tuple(place)].set(smallest).at[tuple(beside)].set(largest)


def block_levels(rng, dims, split, least, largest):
    factor_of, own = 1.0, jax.random.fold_in(rng, 6)
    for dim, shards_of in split:
        draws = jnp.exp(jax.random.uniform(jax.random.fold_in(own, dim), (shards_of,), jnp.float32, least / len(split), largest / len(split)))
        factor_of = factor_of * jnp.repeat(draws, dims[dim] // shards_of).reshape([-1 if axis == dim else 1 for axis in range(len(dims))])
    return factor_of


def normal_values(own_key, shape, scale, reach, split=(), kind=jnp.bfloat16):
    values = jax.random.normal(own_key, shape, jnp.float32) * scale
    if len(split) > 0:
        values = block_levels(own_key, shape, split, -0.22, 0.18) * values
    return jnp.clip(values, min=-reach, max=reach).astype(kind)


def setup_inputs(seed: int = 0) -> dict:
    splits = jax.random.split(jax.random.key(seed), 9)
    amplitudes = normal_values(splits[0], (OCC_OWNED, OCC_SLAB, VIRTUALS, VIRTUALS), 0.5, 4.0, ((0, 2), (1, 32), (2, 4)))
    vv_factors = normal_values(splits[1], (AUXILIARY, VIRTUALS, VIRTUALS), (VIRTUALS * max(1, AUX_DEV // 6)) ** -0.5, 0.25, ((0, 32),))
    ov_factors = normal_values(splits[2], (AUXILIARY, OCC_SLAB, VIRTUALS), (VIRTUALS // 4) ** -0.5, 0.75, ((1, 32),))
    occ_energy_i = jnp.clip(-2.0 + 1.5 * jax.random.uniform(splits[3], (OCC_OWNED,), jnp.float32) ** block_levels(splits[3], (OCC_OWNED,), ((0, 2),), -0.2, 0.2), -2.0, -0.5)
    occ_energy_j = jnp.clip(-2.0 + 1.5 * jax.random.uniform(splits[4], (OCC_SLAB,), jnp.float32) ** block_levels(splits[4], (OCC_SLAB,), ((0, 32),), -0.2, 0.2), -2.0, -0.5)
    virt_energy = jnp.clip(jax.random.uniform(splits[5], (VIRTUALS,), jnp.float32, 0.2, 3.0), 0.2, 3.0)
    vv_mask = plant((jax.random.randint(splits[6], (TILES, TILES), 0, 4) < 3).astype(jnp.int32), jax.random.fold_in(splits[6], 1), 0, 1)
    pair_domain = plant((jax.random.randint(splits[7], (OCC_OWNED, OCC_SLAB, TILES), 0, 4) < 3).astype(jnp.int32), jax.random.fold_in(splits[7], 1), 0, 1)
    return dict(amplitudes=amplitudes, vv_factors=vv_factors, ov_factors=ov_factors, occ_energy_i=occ_energy_i, occ_energy_j=occ_energy_j, virt_energy=virt_energy, vv_mask=vv_mask, pair_domain=pair_domain)


def reference(amplitudes, vv_factors, ov_factors, occ_energy_i, occ_energy_j, virt_energy, vv_mask, pair_domain):
    domain = jnp.repeat(pair_domain, TILE_SIZE, axis=2).astype(jnp.float32)
    pair_mask = domain[:, :, :, None] * domain[:, :, None, :]
    masked = (amplitudes.astype(jnp.float32) * pair_mask).astype(jnp.bfloat16)
    grid = jnp.repeat(jnp.repeat(vv_mask, TILE_SIZE, axis=0), TILE_SIZE, axis=1).astype(jnp.bfloat16)
    factors = vv_factors * grid[None]
    masked_wide = masked.astype(jnp.float32)

    def ladder_step(accum, factor):
        wide = factor.astype(jnp.float32)
        weighted = jnp.einsum('ac,ijcd->ijad', wide, masked_wide).astype(jnp.bfloat16)
        weighted = lax.optimization_barrier(weighted).astype(jnp.float32)
        return accum + jnp.einsum('ijad,bd->ijab', weighted, wide), None

    ladder, unused = lax.scan(ladder_step, jnp.zeros(masked.shape, jnp.float32), factors)
    mixed = (2.0 * masked_wide - jnp.swapaxes(masked_wide, 2, 3)).astype(jnp.bfloat16)
    ov_wide = ov_factors.astype(jnp.float32)
    zeta = jnp.einsum('ikac,qkc->iaq', mixed.astype(jnp.float32), ov_wide)
    cycle = jnp.einsum('iaq,qjb->ijab', zeta, ov_wide, precision=lax.Precision.HIGHEST)
    denom = (virt_energy[None, None, :, None] + virt_energy[None, None, None, :]
             - occ_energy_i[:, None, None, None] - occ_energy_j[None, :, None, None])
    return ((ladder + cycle) * pair_mask / denom).astype(jnp.bfloat16)
```

```python
import jax
import jax.numpy as jnp
from jax import lax
from jax.experimental import pallas as pl
from jax.experimental.pallas import tpu as pltpu
from jax.sharding import Mesh
from jax.sharding import PartitionSpec as P

TILE_SIZE = 128
BF16 = jnp.bfloat16
F32 = jnp.float32
NT = (((1,), (1,)), ((), ()))
TN = (((0,), (0,)), ((), ()))
VIRT = 4
Y = 4
Z = 8


def transposition():
    pairs = []
    for x in range(VIRT):
        for y in range(Y):
            for z in range(Z):
                pairs.append(((x * Y + y) * Z + z, (y * Y + x) * Z + z))
    return pairs


def zeta_kernel(rows_ref, ov_ref, out_ref):
    total = jnp.zeros(out_ref.shape, F32)
    for k in range(Z):
        amp = rows_ref[:, k].reshape(256, 256)
        fac = ov_ref[k]
        direct = lax.dot_general(fac, amp, NT, preferred_element_type=F32)
        swapped = jnp.dot(fac, amp, preferred_element_type=F32)
        total = total + (2.0 * direct - swapped)
    out_ref[...] = total


def ladder_kernel(mask_ref, rows_ref, factors_ref, zeta_ref, ov_ref, out_ref, masked, weighted):
    n_aux = factors_ref.shape[0]

    @pl.when(pl.program_id(0) == 0)
    def _():
        for p in range(2):
            for q in range(2):
                keep = jnp.full((1, TILE_SIZE), mask_ref[p, q], jnp.int32).astype(F32).astype(BF16)
                for aux in range(n_aux):
                    block = factors_ref[aux, p * 128 : (p + 1) * 128, q * 128 : (q + 1) * 128] * keep
                    masked[p * 128 : (p + 1) * 128, aux * 256 + q * 128 : aux * 256 + (q + 1) * 128] = block

    amp = rows_ref[...].reshape(256, 256)
    for aux in range(n_aux):
        cols = slice(aux * 256, (aux + 1) * 256)
        weighted[:, cols] = jnp.dot(masked[:, cols], amp, preferred_element_type=F32).astype(BF16)
    total = lax.dot_general(weighted[...], masked[...], NT, preferred_element_type=F32)
    zeta = zeta_ref[0]
    for other in range(1, VIRT):
        zeta = zeta + zeta_ref[other]
    upper = zeta.astype(BF16)
    lower = (zeta - upper.astype(F32)).astype(BF16)
    fac = ov_ref[0]
    total = total + lax.dot_general(upper, fac, TN, preferred_element_type=F32)
    total = total + lax.dot_general(lower, fac, TN, preferred_element_type=F32)
    out_ref[...] = total.astype(BF16).reshape(out_ref.shape)


def body(
    amplitudes,
    vv_factors,
    ov_factors,
    occ_energy_i,
    occ_energy_j,
    virt_energy,
    vv_mask,
    pair_domain,
):
    share = amplitudes.shape[2]
    virtuals = amplitudes.shape[3]
    n_aux = vv_factors.shape[0]
    virt_index = lax.axis_index("virt")
    row_start = virt_index * share
    domain = jnp.repeat(pair_domain[0, 0], TILE_SIZE).astype(F32)
    domain_rows = lax.dynamic_slice_in_dim(domain, row_start, share, 0)
    masked = (amplitudes[0, 0].astype(F32) * domain_rows[:, None] * domain[None, :]).astype(BF16)
    ov_share = lax.dynamic_slice_in_dim(ov_factors[:, 0, :], virt_index * (n_aux * Z), n_aux * Z, 0)
    swap = transposition()
    payload = jnp.concatenate([masked, ov_share], axis=0)
    payload = lax.ppermute(payload, ("virt", "y", "z"), swap)
    rows = jnp.broadcast_to(payload[None, :share], (Z, share, virtuals))
    parts = payload[share:].reshape(Z, n_aux, virtuals)
    sent = jnp.concatenate([rows, parts], axis=1)
    got = lax.all_to_all(sent, "z", 0, 0, tiled=True)
    rows = got[:, :share]
    ov = got[:, share:]
    rows = lax.all_to_all(jnp.broadcast_to(rows[None], (Y,) + rows.shape), "y", 0, 0, tiled=True)

    zeta = pl.pallas_call(
        zeta_kernel,
        name="zeta",
        out_shape=jax.ShapeDtypeStruct((n_aux, virtuals), F32),
        compiler_params=pltpu.CompilerParams(vmem_limit_bytes=16 << 20),
    )(rows, ov)
    zeta = lax.all_to_all(jnp.broadcast_to(zeta[None], (VIRT, n_aux, virtuals)), "virt", 0, 0, tiled=True)

    partial = pl.pallas_call(
        ladder_kernel,
        name="ladder",
        grid=(Z,),
        in_specs=[
            pl.BlockSpec(memory_space=pltpu.SMEM),
            pl.BlockSpec((Y, 1, share, virtuals), lambda j: (0, j, 0, 0)),
            pl.BlockSpec((n_aux, virtuals, virtuals), lambda j: (0, 0, 0)),
            pl.BlockSpec((VIRT, n_aux, virtuals), lambda j: (0, 0, 0)),
            pl.BlockSpec((1, n_aux, virtuals), lambda j: (j, 0, 0)),
        ],
        out_specs=pl.BlockSpec((Y, 1, share, virtuals), lambda j: (0, j, 0, 0)),
        out_shape=jax.ShapeDtypeStruct((Y, Z, share, virtuals), BF16),
        scratch_shapes=[
            pltpu.VMEM((virtuals, n_aux * virtuals), BF16),
            pltpu.VMEM((virtuals, n_aux * virtuals), BF16),
        ],
        compiler_params=pltpu.CompilerParams(vmem_limit_bytes=40 << 20),
    )(vv_mask, rows, vv_factors, zeta, ov)

    moved = lax.all_to_all(partial, "y", 0, 0, tiled=True)
    summed = jnp.sum(moved.astype(F32), axis=0).astype(BF16)
    moved = lax.all_to_all(summed, "z", 0, 0, tiled=True)
    total = jnp.sum(moved.astype(F32), axis=0).astype(BF16)
    total = lax.ppermute(total, ("virt", "y", "z"), swap).astype(F32)

    energy_rows = lax.dynamic_slice_in_dim(virt_energy, row_start, share, 0)
    denom = energy_rows[:, None] + virt_energy[None, :] - occ_energy_i[0] - occ_energy_j[0]
    update = (total * domain_rows[:, None] * domain[None, :] / denom).astype(BF16)
    return update[None, None]


def solution(mesh):
    fine = Mesh(mesh.devices.reshape(2, VIRT, Y, Z), ("pair", "virt", "y", "z"))
    integ = ("y", "z")
    placed = (
        P("pair", integ, "virt", None),
        P(integ, None, None),
        P(None, integ, None),
        P("pair"),
        P(integ),
        P(),
        P(),
        P("pair", integ, None),
    )
    return jax.shard_map(
        body,
        mesh=fine,
        in_specs=placed,
        out_specs=P("pair", integ, "virt", None),
        check_vma=False,
    )
```

```python
import jax
import jax.numpy as jnp
from jax import lax
from jax.experimental import pallas as pl
from jax.experimental.pallas import tpu as pltpu
from jax.sharding import Mesh
from jax.sharding import PartitionSpec as P

TILE_SIZE = 128
BF16 = jnp.bfloat16
F32 = jnp.float32
NT = (((1,), (1,)), ((), ()))
TN = (((0,), (0,)), ((), ()))
VIRT = 4
Y = 4
Z = 8
ROWS = 64
COLS = 256
AUX = 16


def out_kernel(domain_ref, amp_ref, ov_ref, out_ref):
    x = lax.axis_index("virt")
    z = lax.axis_index("z")
    row_tile = domain_ref[0, 0, x // 2]
    for half in range(2):
        cols = slice(half * TILE_SIZE, (half + 1) * TILE_SIZE)
        keep = (row_tile * domain_ref[0, 0, half]).astype(F32)
        rows = (amp_ref[0, 0, :, cols].astype(F32) * keep).astype(BF16)
        for to in range(Z):
            out_ref[to, :ROWS, cols] = rows
    owner = (x + Y - z % 2) % Y
    start = pl.multiple_of(owner * (Z * AUX), Z * AUX)
    out_ref[:, ROWS:] = ov_ref[pl.ds(start, Z * AUX), :].reshape(Z, AUX, COLS)


def spread_kernel(got_ref, out_ref):
    x = lax.axis_index("virt")
    for to_x in range(VIRT):
        rows = got_ref[2 * to_x : 2 * to_x + 2, :ROWS].reshape(2 * ROWS, COLS)
        for to_y in range(Y):
            out_ref[to_x * Y + to_y, : 2 * ROWS] = rows
            low = (x + Y - to_y) % 2
            out_ref[to_x * Y + to_y, 2 * ROWS :] = got_ref[2 * to_x + low, ROWS:]


def ladder_kernel(mask_ref, rows_ref, factors_ref, out_ref, masked, weighted):
    y = lax.axis_index("y")
    for p in range(2):
        for q in range(2):
            keep = jnp.full((1, TILE_SIZE), mask_ref[p, q], jnp.int32).astype(F32).astype(BF16)
            for aux in range(AUX):
                block = factors_ref[aux, p * 128 : (p + 1) * 128, q * 128 : (q + 1) * 128] * keep
                masked[p * 128 : (p + 1) * 128, aux * 256 + q * 128 : aux * 256 + (q + 1) * 128] = block

    zeta = jnp.zeros((AUX, COLS), F32)
    for at_y in range(Y):
        for low in range(2):
            rows = slice(low * ROWS, (low + 1) * ROWS)
            amp = jnp.concatenate([rows_ref[at_x * Y + at_y, rows] for at_x in range(VIRT)], axis=0)
            fac = rows_ref[((y + low) % Y) * Y + at_y, 2 * ROWS :]
            direct = lax.dot_general(fac, amp, NT, preferred_element_type=F32)
            swapped = jnp.dot(fac, amp, preferred_element_type=F32)
            zeta = zeta + (2.0 * direct - swapped)
            for aux in range(AUX):
                cols = slice(aux * 256, (aux + 1) * 256)
                weighted[:, cols] = jnp.dot(masked[:, cols], amp, preferred_element_type=F32).astype(BF16)
            total = lax.dot_general(weighted[...], masked[...], NT, preferred_element_type=F32).astype(BF16)
            for at_x in range(VIRT):
                out_ref[at_x * Y + at_y, rows] = total[at_x * ROWS : (at_x + 1) * ROWS]
    lane = lax.broadcasted_iota(jnp.int32, (AUX, COLS), 1)
    for at_x in range(VIRT):
        turned = pltpu.roll(zeta, ((y + VIRT - at_x) % VIRT) * ROWS, 1)
        piece = jnp.where(lane // ROWS == y, turned, 0.0).astype(BF16)
        for at_y in range(Y):
            out_ref[at_x * Y + at_y, 2 * ROWS :] = piece


def sum_kernel(got_ref, out_ref):
    for high in range(VIRT):
        for low in range(2):
            rows = slice(low * ROWS, (low + 1) * ROWS)
            total = got_ref[high * Y, rows].astype(F32)
            for at_y in range(1, Y):
                total = total + got_ref[high * Y + at_y, rows].astype(F32)
            out_ref[2 * high + low, :ROWS] = total.astype(BF16)
    zeta = jnp.zeros((AUX, COLS), F32)
    for source in range(VIRT * Y):
        zeta = zeta + got_ref[source, 2 * ROWS :].astype(F32)
    zeta = zeta.astype(BF16)
    for to in range(Z):
        out_ref[to, ROWS:] = zeta


def update_kernel(domain_ref, occ_i_ref, occ_j_ref, virt_ref, got_ref, ov_ref, out_ref):
    x = lax.axis_index("virt")
    total = got_ref[0, :ROWS].astype(F32)
    for source in range(1, Z):
        total = total + got_ref[source, :ROWS].astype(F32)
    zeta = got_ref[:, ROWS:].reshape(Z * AUX, COLS)
    for at_y in range(Y):
        part = zeta[:, at_y * ROWS : (at_y + 1) * ROWS]
        fac = ov_ref[at_y * Z * AUX : (at_y + 1) * Z * AUX, :]
        total = total + lax.dot_general(part, fac, TN, preferred_element_type=F32)
    energy = jnp.broadcast_to(virt_ref[...], (ROWS, COLS))
    row = lax.broadcasted_iota(jnp.int32, (ROWS, COLS), 0) + x * ROWS
    lane = lax.broadcasted_iota(jnp.int32, (ROWS, COLS), 1)
    energy_rows = jnp.sum(jnp.where(row == lane, energy, 0.0), axis=1, keepdims=True)
    denom = energy_rows + energy - occ_i_ref[0] - occ_j_ref[0]
    row_tile = domain_ref[0, 0, x // 2]
    left = (row_tile * domain_ref[0, 0, 0]).astype(F32)
    right = (row_tile * domain_ref[0, 0, 1]).astype(F32)
    keep = jnp.where(lane < TILE_SIZE, left, right)
    out_ref[0, 0] = (total * keep / denom).astype(BF16)


def kernel(function, shape, scalars, arrays, scratch=(), mib=16):
    smem = pl.BlockSpec(memory_space=pltpu.SMEM)
    vmem = pl.BlockSpec(memory_space=pltpu.VMEM)
    call = pl.pallas_call(
        function,
        name=function.__name__,
        in_specs=[smem] * len(scalars) + [vmem] * len(arrays),
        out_specs=vmem,
        out_shape=jax.ShapeDtypeStruct(shape, BF16),
        scratch_shapes=list(scratch),
        compiler_params=pltpu.CompilerParams(vmem_limit_bytes=mib << 20),
    )
    return call(*scalars, *arrays)


def body(
    amplitudes,
    vv_factors,
    ov_factors,
    occ_energy_i,
    occ_energy_j,
    virt_energy,
    vv_mask,
    pair_domain,
):
    ov = ov_factors[:, 0, :]
    sent = kernel(out_kernel, (Z, ROWS + AUX, COLS), (pair_domain,), (amplitudes, ov))
    got = lax.all_to_all(sent, "z", 0, 0, tiled=True)
    sent = kernel(spread_kernel, (VIRT * Y, 2 * ROWS + AUX, COLS), (), (got,))
    got = lax.all_to_all(sent, ("virt", "y"), 0, 0, tiled=True)
    wide = pltpu.VMEM((COLS, AUX * COLS), BF16)
    sent = kernel(ladder_kernel, (VIRT * Y, 2 * ROWS + AUX, COLS), (vv_mask,), (got, vv_factors), (wide, wide), 40)
    got = lax.all_to_all(sent, ("virt", "y"), 0, 0, tiled=True)
    sent = kernel(sum_kernel, (Z, ROWS + AUX, COLS), (), (got,))
    got = lax.all_to_all(sent, "z", 0, 0, tiled=True)
    return kernel(
        update_kernel,
        (1, 1, ROWS, COLS),
        (pair_domain, occ_energy_i, occ_energy_j),
        (virt_energy[None, :], got, ov),
    )


def solution(mesh):
    fine = Mesh(mesh.devices.reshape(2, VIRT, Y, Z), ("pair", "virt", "y", "z"))
    integ = ("y", "z")
    placed = (
        P("pair", integ, "virt", None),
        P(integ, None, None),
        P(None, integ, None),
        P("pair"),
        P(integ),
        P(),
        P(),
        P("pair", integ, None),
    )
    return jax.shard_map(
        body,
        mesh=fine,
        in_specs=placed,
        out_specs=P("pair", integ, "virt", None),
        check_vma=False,
    )
```

```python
import jax
import jax.numpy as jnp
from jax import lax
from jax.experimental import pallas as pl
from jax.experimental.pallas import tpu as pltpu
from jax.sharding import Mesh
from jax.sharding import PartitionSpec as P

TILE_SIZE = 128
BF16 = jnp.bfloat16
F32 = jnp.float32
NT = (((1,), (1,)), ((), ()))
TN = (((0,), (0,)), ((), ()))
VIRT = 4
Y = 4
Z = 8
ROWS = 64
COLS = 256
AUX = 16


def out_kernel(domain_hbm, amp_hbm, ov_hbm, out_ref, domain, amp, sems):
    x = lax.axis_index("virt")
    z = lax.axis_index("z")
    owner = (x + Y - z % 2) % Y
    copies = [
        pltpu.make_async_copy(domain_hbm.at[0], domain, sems.at[0]),
        pltpu.make_async_copy(amp_hbm.at[0, 0], amp, sems.at[1]),
    ]
    for to in range(Z):
        start = pl.multiple_of((owner * Z + to) * AUX, AUX)
        copies.append(pltpu.make_async_copy(ov_hbm.at[pl.ds(start, AUX)], out_ref.at[to, pl.ds(ROWS, AUX)], sems.at[2 + to]))
    for copy in copies:
        copy.start()
    copies[0].wait()
    copies[1].wait()
    row_tile = domain[0, x // 2]
    for half in range(2):
        cols = slice(half * TILE_SIZE, (half + 1) * TILE_SIZE)
        keep = (row_tile * domain[0, half]).astype(F32)
        rows = (amp[:, cols].astype(F32) * keep).astype(BF16)
        for to in range(Z):
            out_ref[to, :ROWS, cols] = rows
    for copy in copies[2:]:
        copy.wait()


def spread_kernel(got_ref, out_ref):
    x = lax.axis_index("virt")
    for to_x in range(VIRT):
        rows = got_ref[2 * to_x : 2 * to_x + 2, :ROWS].reshape(2 * ROWS, COLS)
        for to_y in range(Y):
            out_ref[to_x * Y + to_y, : 2 * ROWS] = rows
            low = (x + Y - to_y) % 2
            out_ref[to_x * Y + to_y, 2 * ROWS :] = got_ref[2 * to_x + low, ROWS:]


def ladder_kernel(mask_ref, rows_ref, factors_ref, out_ref, masked, weighted):
    y = lax.axis_index("y")
    for p in range(2):
        for q in range(2):
            keep = jnp.full((1, TILE_SIZE), mask_ref[p, q], jnp.int32).astype(F32).astype(BF16)
            for aux in range(AUX):
                block = factors_ref[aux, p * 128 : (p + 1) * 128, q * 128 : (q + 1) * 128] * keep
                masked[p * 128 : (p + 1) * 128, aux * 256 + q * 128 : aux * 256 + (q + 1) * 128] = block

    zeta = jnp.zeros((AUX, COLS), F32)
    for at_y in range(Y):
        for low in range(2):
            rows = slice(low * ROWS, (low + 1) * ROWS)
            amp = jnp.concatenate([rows_ref[at_x * Y + at_y, rows] for at_x in range(VIRT)], axis=0)
            fac = rows_ref[((y + low) % Y) * Y + at_y, 2 * ROWS :]
            direct = lax.dot_general(fac, amp, NT, preferred_element_type=F32)
            swapped = jnp.dot(fac, amp, preferred_element_type=F32)
            zeta = zeta + (2.0 * direct - swapped)
            for aux in range(AUX):
                cols = slice(aux * 256, (aux + 1) * 256)
                weighted[:, cols] = jnp.dot(masked[:, cols], amp, preferred_element_type=F32).astype(BF16)
            total = lax.dot_general(weighted[...], masked[...], NT, preferred_element_type=F32).astype(BF16)
            for at_x in range(VIRT):
                out_ref[at_x * Y + at_y, rows] = total[at_x * ROWS : (at_x + 1) * ROWS]
    lane = lax.broadcasted_iota(jnp.int32, (AUX, COLS), 1)
    for at_x in range(VIRT):
        turned = pltpu.roll(zeta, ((y + VIRT - at_x) % VIRT) * ROWS, 1)
        piece = jnp.where(lane // ROWS == y, turned, 0.0).astype(BF16)
        for at_y in range(Y):
            out_ref[at_x * Y + at_y, 2 * ROWS :] = piece


def sum_kernel(got_ref, out_ref):
    for high in range(VIRT):
        for low in range(2):
            rows = slice(low * ROWS, (low + 1) * ROWS)
            total = got_ref[high * Y, rows].astype(F32)
            for at_y in range(1, Y):
                total = total + got_ref[high * Y + at_y, rows].astype(F32)
            out_ref[2 * high + low, :ROWS] = total.astype(BF16)
    zeta = jnp.zeros((AUX, COLS), F32)
    for source in range(VIRT * Y):
        zeta = zeta + got_ref[source, 2 * ROWS :].astype(F32)
    zeta = zeta.astype(BF16)
    for to in range(Z):
        out_ref[to, ROWS:] = zeta


def update_kernel(domain_ref, occ_i_ref, occ_j_ref, virt_ref, got_ref, ov_ref, out_ref):
    x = lax.axis_index("virt")
    total = got_ref[0, :ROWS].astype(F32)
    for source in range(1, Z):
        total = total + got_ref[source, :ROWS].astype(F32)
    zeta = got_ref[:, ROWS:].reshape(Z * AUX, COLS)
    for at_y in range(Y):
        part = zeta[:, at_y * ROWS : (at_y + 1) * ROWS]
        fac = ov_ref[at_y * Z * AUX : (at_y + 1) * Z * AUX, :]
        total = total + lax.dot_general(part, fac, TN, preferred_element_type=F32)
    energy = jnp.broadcast_to(virt_ref[...], (ROWS, COLS))
    row = lax.broadcasted_iota(jnp.int32, (ROWS, COLS), 0) + x * ROWS
    lane = lax.broadcasted_iota(jnp.int32, (ROWS, COLS), 1)
    energy_rows = jnp.sum(jnp.where(row == lane, energy, 0.0), axis=1, keepdims=True)
    denom = energy_rows + energy - occ_i_ref[0] - occ_j_ref[0]
    row_tile = domain_ref[0, 0, x // 2]
    left = (row_tile * domain_ref[0, 0, 0]).astype(F32)
    right = (row_tile * domain_ref[0, 0, 1]).astype(F32)
    keep = jnp.where(lane < TILE_SIZE, left, right)
    out_ref[0, 0] = (total * keep / denom).astype(BF16)


def kernel(function, shape, scalars, arrays, scratch=(), mib=16):
    smem = pl.BlockSpec(memory_space=pltpu.SMEM)
    vmem = pl.BlockSpec(memory_space=pltpu.VMEM)
    call = pl.pallas_call(
        function,
        name=function.__name__,
        in_specs=[smem] * len(scalars) + [vmem] * len(arrays),
        out_specs=vmem,
        out_shape=jax.ShapeDtypeStruct(shape, BF16),
        scratch_shapes=list(scratch),
        compiler_params=pltpu.CompilerParams(vmem_limit_bytes=mib << 20),
    )
    return call(*scalars, *arrays)


def body(
    amplitudes,
    vv_factors,
    ov_factors,
    occ_energy_i,
    occ_energy_j,
    virt_energy,
    vv_mask,
    pair_domain,
):
    ov = ov_factors[:, 0, :]
    hbm = pl.BlockSpec(memory_space=pltpu.HBM)
    sent = pl.pallas_call(
        out_kernel,
        name="out_kernel",
        in_specs=[hbm, hbm, hbm],
        out_specs=pl.BlockSpec(memory_space=pltpu.VMEM),
        out_shape=jax.ShapeDtypeStruct((Z, ROWS + AUX, COLS), BF16),
        scratch_shapes=[
            pltpu.SMEM((1, 2), jnp.int32),
            pltpu.VMEM((ROWS, COLS), BF16),
            pltpu.SemaphoreType.DMA((2 + Z,)),
        ],
    )(pair_domain, amplitudes, ov)
    got = lax.all_to_all(sent, "z", 0, 0, tiled=True)
    sent = kernel(spread_kernel, (VIRT * Y, 2 * ROWS + AUX, COLS), (), (got,))
    got = lax.all_to_all(sent, ("virt", "y"), 0, 0, tiled=True)
    wide = pltpu.VMEM((COLS, AUX * COLS), BF16)
    sent = kernel(ladder_kernel, (VIRT * Y, 2 * ROWS + AUX, COLS), (vv_mask,), (got, vv_factors), (wide, wide), 40)
    got = lax.all_to_all(sent, ("virt", "y"), 0, 0, tiled=True)
    sent = kernel(sum_kernel, (Z, ROWS + AUX, COLS), (), (got,))
    got = lax.all_to_all(sent, "z", 0, 0, tiled=True)
    return kernel(
        update_kernel,
        (1, 1, ROWS, COLS),
        (pair_domain, occ_energy_i, occ_energy_j),
        (virt_energy[None, :], got, ov),
    )


def solution(mesh):
    fine = Mesh(mesh.devices.reshape(2, VIRT, Y, Z), ("pair", "virt", "y", "z"))
    integ = ("y", "z")
    placed = (
        P("pair", integ, "virt", None),
        P(integ, None, None),
        P(None, integ, None),
        P("pair"),
        P(integ),
        P(),
        P(),
        P("pair", integ, None),
    )
    return jax.shard_map(
        body,
        mesh=fine,
        in_specs=placed,
        out_specs=P("pair", integ, "virt", None),
        check_vma=False,
    )
```

```python
import jax
import jax.numpy as jnp
from jax import lax
from jax.experimental import pallas as pl
from jax.experimental.pallas import tpu as pltpu
from jax.sharding import Mesh
from jax.sharding import PartitionSpec as P

TILE_SIZE = 128
BF16 = jnp.bfloat16
F32 = jnp.float32
NT = (((1,), (1,)), ((), ()))
TN = (((0,), (0,)), ((), ()))
VIRT = 4
Y = 4
Z = 8
ROWS = 64
COLS = 256
AUX = 16
PART = 8


def out_kernel(domain_hbm, amp_hbm, ov_hbm, out_ref, domain, amp, sems):
    x = lax.axis_index("virt")
    copies = [
        pltpu.make_async_copy(domain_hbm.at[0], domain, sems.at[0]),
        pltpu.make_async_copy(amp_hbm.at[0, 0], amp, sems.at[1]),
    ]
    for to in range(Z):
        for high in range(2):
            start = pl.multiple_of(((2 * high + x // 2) * Z + to) * AUX + (x % 2) * PART, PART)
            target = out_ref.at[to, pl.ds(ROWS + high * PART, PART)]
            copies.append(pltpu.make_async_copy(ov_hbm.at[pl.ds(start, PART)], target, sems.at[2 + 2 * to + high]))
    for copy in copies:
        copy.start()
    copies[0].wait()
    copies[1].wait()
    row_tile = domain[0, x // 2]
    for half in range(2):
        cols = slice(half * TILE_SIZE, (half + 1) * TILE_SIZE)
        keep = (row_tile * domain[0, half]).astype(F32)
        rows = (amp[:, cols].astype(F32) * keep).astype(BF16)
        for to in range(Z):
            out_ref[to, :ROWS, cols] = rows
    for copy in copies[2:]:
        copy.wait()


def spread_kernel(got_ref, out_ref):
    for to_x in range(VIRT):
        for to_y in range(Y):
            high, low = divmod(to_y, 2)
            out_ref[to_x * Y + to_y, :ROWS] = got_ref[2 * to_x + low, :ROWS]
            start = ROWS + high * PART
            out_ref[to_x * Y + to_y, ROWS:] = got_ref[2 * to_x + low, start : start + PART]


def ladder_kernel(mask_ref, rows_ref, own_ref, near_ref, far_ref, out_ref, masked, weighted):
    sources = [(own_ref, aux) for aux in range(AUX)]
    sources += [(ref, aux) for ref in (near_ref, far_ref) for aux in range(PART)]
    for p in range(2):
        for q in range(2):
            keep = jnp.full((1, TILE_SIZE), mask_ref[p, q], jnp.int32).astype(F32).astype(BF16)
            for slot, (ref, aux) in enumerate(sources):
                block = ref[aux, p * 128 : (p + 1) * 128, q * 128 : (q + 1) * 128] * keep
                masked[p * 128 : (p + 1) * 128, slot * 256 + q * 128 : slot * 256 + (q + 1) * 128] = block

    zeta = jnp.zeros((2 * AUX, COLS), F32)
    for at_y in range(Y):
        amp = jnp.concatenate([rows_ref[at_x * Y + at_y, :ROWS] for at_x in range(VIRT)], axis=0)
        fac = jnp.concatenate([rows_ref[at_x * Y + at_y, ROWS:] for at_x in range(VIRT)], axis=0)
        direct = lax.dot_general(fac, amp, NT, preferred_element_type=F32)
        swapped = jnp.dot(fac, amp, preferred_element_type=F32)
        zeta = zeta + (2.0 * direct - swapped)
        for slot in range(2 * AUX):
            cols = slice(slot * 256, (slot + 1) * 256)
            weighted[:, cols] = jnp.dot(masked[:, cols], amp, preferred_element_type=F32).astype(BF16)
        total = lax.dot_general(weighted[...], masked[...], NT, preferred_element_type=F32).astype(BF16)
        for at_x in range(VIRT):
            out_ref[at_x * Y + at_y, :ROWS] = total[at_x * ROWS : (at_x + 1) * ROWS]
    group = lax.broadcasted_iota(jnp.int32, (PART, COLS), 1) // ROWS
    for at_x in range(VIRT):
        piece = jnp.zeros((PART, COLS), F32)
        for to in range(4):
            turned = zeta[to * PART : (to + 1) * PART]
            if to != at_x:
                turned = pltpu.roll(turned, ((to - at_x) % 4) * ROWS, 1)
            piece = jnp.where(group == to, turned, piece)
        piece = piece.astype(BF16)
        for at_y in range(Y):
            out_ref[at_x * Y + at_y, ROWS:] = piece


def sum_kernel(got_ref, out_ref):
    sums = [jnp.zeros((PART, COLS), F32), jnp.zeros((PART, COLS), F32)]
    for at_x in range(VIRT):
        for low in range(2):
            first = got_ref[at_x * Y + low]
            second = got_ref[at_x * Y + 2 + low]
            out_ref[2 * at_x + low, :ROWS] = (first[:ROWS].astype(F32) + second[:ROWS].astype(F32)).astype(BF16)
            sums[0] = sums[0] + first[ROWS:].astype(F32)
            sums[1] = sums[1] + second[ROWS:].astype(F32)
    group = lax.broadcasted_iota(jnp.int32, (PART, COLS), 1) // ROWS
    halves = []
    for half in range(2):
        piece = jnp.zeros((PART, COLS), F32)
        for high in range(2):
            for low in range(2):
                source, to = 2 * low + half, 2 * high + low
                turned = sums[high]
                if source != to:
                    turned = pltpu.roll(turned, ((to - source) % 4) * ROWS, 1)
                piece = jnp.where(group == to, turned, piece)
        halves.append(piece)
    zeta = jnp.concatenate(halves, axis=0).astype(BF16)
    for to in range(Z):
        out_ref[to, ROWS:] = zeta


def update_kernel(domain_ref, occ_i_ref, occ_j_ref, virt_ref, got_ref, ov_ref, out_ref):
    x = lax.axis_index("virt")
    total = got_ref[0, :ROWS].astype(F32)
    for source in range(1, Z):
        total = total + got_ref[source, :ROWS].astype(F32)
    zeta = got_ref[:, ROWS:].reshape(Z * AUX, COLS)
    for at_y in range(Y):
        part = zeta[:, at_y * ROWS : (at_y + 1) * ROWS]
        fac = ov_ref[at_y * Z * AUX : (at_y + 1) * Z * AUX, :]
        total = total + lax.dot_general(part, fac, TN, preferred_element_type=F32)
    energy = jnp.broadcast_to(virt_ref[...], (ROWS, COLS))
    row = lax.broadcasted_iota(jnp.int32, (ROWS, COLS), 0) + x * ROWS
    lane = lax.broadcasted_iota(jnp.int32, (ROWS, COLS), 1)
    energy_rows = jnp.sum(jnp.where(row == lane, energy, 0.0), axis=1, keepdims=True)
    denom = energy_rows + energy - occ_i_ref[0] - occ_j_ref[0]
    row_tile = domain_ref[0, 0, x // 2]
    left = (row_tile * domain_ref[0, 0, 0]).astype(F32)
    right = (row_tile * domain_ref[0, 0, 1]).astype(F32)
    keep = jnp.where(lane < TILE_SIZE, left, right)
    out_ref[0, 0] = (total * keep / denom).astype(BF16)


def kernel(function, shape, scalars, arrays, scratch=(), mib=16):
    smem = pl.BlockSpec(memory_space=pltpu.SMEM)
    vmem = pl.BlockSpec(memory_space=pltpu.VMEM)
    call = pl.pallas_call(
        function,
        name=function.__name__,
        in_specs=[smem] * len(scalars) + [vmem] * len(arrays),
        out_specs=vmem,
        out_shape=jax.ShapeDtypeStruct(shape, BF16),
        scratch_shapes=list(scratch),
        compiler_params=pltpu.CompilerParams(vmem_limit_bytes=mib << 20),
    )
    return call(*scalars, *arrays)


def body(
    amplitudes,
    vv_factors,
    ov_factors,
    occ_energy_i,
    occ_energy_j,
    virt_energy,
    vv_mask,
    pair_domain,
):
    ov = ov_factors[:, 0, :]
    mine = lax.dynamic_slice_in_dim(vv_factors, lax.axis_index("pair") * PART, PART, 0)
    hbm = pl.BlockSpec(memory_space=pltpu.HBM)
    sent = pl.pallas_call(
        out_kernel,
        name="out_kernel",
        in_specs=[hbm, hbm, hbm],
        out_specs=pl.BlockSpec(memory_space=pltpu.VMEM),
        out_shape=jax.ShapeDtypeStruct((Z, ROWS + AUX, COLS), BF16),
        scratch_shapes=[
            pltpu.SMEM((1, 2), jnp.int32),
            pltpu.VMEM((ROWS, COLS), BF16),
            pltpu.SemaphoreType.DMA((2 + 2 * Z,)),
        ],
    )(pair_domain, amplitudes, ov)
    got = lax.all_to_all(sent, "z", 0, 0, tiled=True)
    sent = kernel(spread_kernel, (VIRT * Y, ROWS + PART, COLS), (), (got,))
    near = lax.ppermute(mine, "y", [(y, y ^ 1) for y in range(Y)])
    far = lax.ppermute(near, "pair", [(0, 1), (1, 0)])
    got = lax.all_to_all(sent, ("virt", "y"), 0, 0, tiled=True)
    wide = pltpu.VMEM((COLS, 2 * AUX * COLS), BF16)
    sent = kernel(
        ladder_kernel,
        (VIRT * Y, ROWS + PART, COLS),
        (vv_mask,),
        (got, vv_factors, near, far),
        (wide, wide),
        40,
    )
    got = lax.all_to_all(sent, ("virt", "y"), 0, 0, tiled=True)
    sent = kernel(sum_kernel, (Z, ROWS + AUX, COLS), (), (got,))
    got = lax.all_to_all(sent, "z", 0, 0, tiled=True)
    return kernel(
        update_kernel,
        (1, 1, ROWS, COLS),
        (pair_domain, occ_energy_i, occ_energy_j),
        (virt_energy[None, :], got, ov),
    )


def solution(mesh):
    fine = Mesh(mesh.devices.reshape(2, VIRT, Y, Z), ("pair", "virt", "y", "z"))
    integ = ("y", "z")
    placed = (
        P("pair", integ, "virt", None),
        P(integ, None, None),
        P(None, integ, None),
        P("pair"),
        P(integ),
        P(),
        P(),
        P("pair", integ, None),
    )
    return jax.shard_map(
        body,
        mesh=fine,
        in_specs=placed,
        out_specs=P("pair", integ, "virt", None),
        check_vma=False,
    )
```

```python
import jax
import jax.numpy as jnp
from jax import lax
from jax.experimental import pallas as pl
from jax.experimental.pallas import tpu as pltpu
from jax.sharding import Mesh
from jax.sharding import PartitionSpec as P

TILE_SIZE = 128
BF16 = jnp.bfloat16
F32 = jnp.float32
NT = (((1,), (1,)), ((), ()))
TN = (((0,), (0,)), ((), ()))
VIRT = 4
Y = 4
Z = 8
ROWS = 64
COLS = 256
AUX = 16
PART = 8
SHARE = 2


def out_kernel(domain_hbm, amp_hbm, ov_hbm, factors_hbm, out_ref, share_ref, domain, amp, sems):
    x = lax.axis_index("virt")
    share = (2 * x + lax.axis_index("pair")) * SHARE
    copies = [
        pltpu.make_async_copy(domain_hbm.at[0], domain, sems.at[0]),
        pltpu.make_async_copy(amp_hbm.at[0, 0], amp, sems.at[1]),
        pltpu.make_async_copy(factors_hbm.at[pl.ds(share, SHARE)], share_ref, sems.at[2]),
    ]
    for to in range(Z):
        for high in range(2):
            start = pl.multiple_of(((2 * high + x // 2) * Z + to) * AUX + (x % 2) * PART, PART)
            target = out_ref.at[to, pl.ds(ROWS + high * PART, PART)]
            copies.append(pltpu.make_async_copy(ov_hbm.at[pl.ds(start, PART)], target, sems.at[3 + 2 * to + high]))
    for copy in copies:
        copy.start()
    copies[0].wait()
    copies[1].wait()
    row_tile = domain[0, x // 2]
    for half in range(2):
        cols = slice(half * TILE_SIZE, (half + 1) * TILE_SIZE)
        keep = (row_tile * domain[0, half]).astype(F32)
        rows = (amp[:, cols].astype(F32) * keep).astype(BF16)
        for to in range(Z):
            out_ref[to, :ROWS, cols] = rows
    for copy in copies[2:]:
        copy.wait()


def spread_kernel(got_ref, out_ref):
    for to_x in range(VIRT):
        for to_y in range(Y):
            high, low = divmod(to_y, 2)
            out_ref[to_x * Y + to_y, :ROWS] = got_ref[2 * to_x + low, :ROWS]
            start = ROWS + high * PART
            out_ref[to_x * Y + to_y, ROWS:] = got_ref[2 * to_x + low, start : start + PART]


def ladder_kernel(mask_ref, rows_ref, own_ref, near_ref, out_ref, masked, weighted):
    sources = [(ref, aux) for ref in (own_ref, near_ref) for aux in range(AUX)]
    for p in range(2):
        for q in range(2):
            keep = jnp.full((1, TILE_SIZE), mask_ref[p, q], jnp.int32).astype(F32).astype(BF16)
            for slot, (ref, aux) in enumerate(sources):
                block = ref[aux, p * 128 : (p + 1) * 128, q * 128 : (q + 1) * 128] * keep
                masked[p * 128 : (p + 1) * 128, slot * 256 + q * 128 : slot * 256 + (q + 1) * 128] = block

    zeta = jnp.zeros((2 * AUX, COLS), F32)
    for at_y in range(Y):
        amp = jnp.concatenate([rows_ref[at_x * Y + at_y, :ROWS] for at_x in range(VIRT)], axis=0)
        fac = jnp.concatenate([rows_ref[at_x * Y + at_y, ROWS:] for at_x in range(VIRT)], axis=0)
        direct = lax.dot_general(fac, amp, NT, preferred_element_type=F32)
        swapped = jnp.dot(fac, amp, preferred_element_type=F32)
        zeta = zeta + (2.0 * direct - swapped)
        for slot in range(2 * AUX):
            cols = slice(slot * 256, (slot + 1) * 256)
            weighted[:, cols] = jnp.dot(masked[:, cols], amp, preferred_element_type=F32).astype(BF16)
        total = lax.dot_general(weighted[...], masked[...], NT, preferred_element_type=F32).astype(BF16)
        for at_x in range(VIRT):
            out_ref[at_x * Y + at_y, :ROWS] = total[at_x * ROWS : (at_x + 1) * ROWS]
    group = lax.broadcasted_iota(jnp.int32, (PART, COLS), 1) // ROWS
    for at_x in range(VIRT):
        piece = jnp.zeros((PART, COLS), F32)
        for to in range(4):
            turned = zeta[to * PART : (to + 1) * PART]
            if to != at_x:
                turned = pltpu.roll(turned, ((to - at_x) % 4) * ROWS, 1)
            piece = jnp.where(group == to, turned, piece)
        piece = piece.astype(BF16)
        for at_y in range(Y):
            out_ref[at_x * Y + at_y, ROWS:] = piece


def sum_kernel(got_ref, out_ref):
    sums = [jnp.zeros((PART, COLS), F32), jnp.zeros((PART, COLS), F32)]
    for at_x in range(VIRT):
        for low in range(2):
            first = got_ref[at_x * Y + low]
            second = got_ref[at_x * Y + 2 + low]
            out_ref[2 * at_x + low, :ROWS] = (first[:ROWS].astype(F32) + second[:ROWS].astype(F32)).astype(BF16)
            sums[0] = sums[0] + first[ROWS:].astype(F32)
            sums[1] = sums[1] + second[ROWS:].astype(F32)
    group = lax.broadcasted_iota(jnp.int32, (PART, COLS), 1) // ROWS
    halves = []
    for half in range(2):
        piece = jnp.zeros((PART, COLS), F32)
        for high in range(2):
            for low in range(2):
                source, to = 2 * low + half, 2 * high + low
                turned = sums[high]
                if source != to:
                    turned = pltpu.roll(turned, ((to - source) % 4) * ROWS, 1)
                piece = jnp.where(group == to, turned, piece)
        halves.append(piece)
    zeta = jnp.concatenate(halves, axis=0).astype(BF16)
    for to in range(Z):
        out_ref[to, ROWS:] = zeta


def update_kernel(domain_ref, occ_i_ref, occ_j_ref, virt_ref, got_ref, ov_ref, out_ref):
    x = lax.axis_index("virt")
    total = got_ref[0, :ROWS].astype(F32)
    for source in range(1, Z):
        total = total + got_ref[source, :ROWS].astype(F32)
    zeta = got_ref[:, ROWS:].reshape(Z * AUX, COLS)
    for at_y in range(Y):
        part = zeta[:, at_y * ROWS : (at_y + 1) * ROWS]
        fac = ov_ref[at_y * Z * AUX : (at_y + 1) * Z * AUX, :]
        total = total + lax.dot_general(part, fac, TN, preferred_element_type=F32)
    energy = jnp.broadcast_to(virt_ref[...], (ROWS, COLS))
    row = lax.broadcasted_iota(jnp.int32, (ROWS, COLS), 0) + x * ROWS
    lane = lax.broadcasted_iota(jnp.int32, (ROWS, COLS), 1)
    energy_rows = jnp.sum(jnp.where(row == lane, energy, 0.0), axis=1, keepdims=True)
    denom = energy_rows + energy - occ_i_ref[0] - occ_j_ref[0]
    row_tile = domain_ref[0, 0, x // 2]
    left = (row_tile * domain_ref[0, 0, 0]).astype(F32)
    right = (row_tile * domain_ref[0, 0, 1]).astype(F32)
    keep = jnp.where(lane < TILE_SIZE, left, right)
    out_ref[0, 0] = (total * keep / denom).astype(BF16)


def kernel(function, shape, scalars, arrays, scratch=(), mib=16):
    smem = pl.BlockSpec(memory_space=pltpu.SMEM)
    vmem = pl.BlockSpec(memory_space=pltpu.VMEM)
    call = pl.pallas_call(
        function,
        name=function.__name__,
        in_specs=[smem] * len(scalars) + [vmem] * len(arrays),
        out_specs=vmem,
        out_shape=jax.ShapeDtypeStruct(shape, BF16),
        scratch_shapes=list(scratch),
        compiler_params=pltpu.CompilerParams(vmem_limit_bytes=mib << 20),
    )
    return call(*scalars, *arrays)


def body(
    amplitudes,
    vv_factors,
    ov_factors,
    occ_energy_i,
    occ_energy_j,
    virt_energy,
    vv_mask,
    pair_domain,
):
    ov = ov_factors[:, 0, :]
    hbm = pl.BlockSpec(memory_space=pltpu.HBM)
    sent, mine = pl.pallas_call(
        out_kernel,
        name="out_kernel",
        in_specs=[hbm, hbm, hbm, hbm],
        out_specs=[pl.BlockSpec(memory_space=pltpu.VMEM)] * 2,
        out_shape=[
            jax.ShapeDtypeStruct((Z, ROWS + AUX, COLS), BF16),
            jax.ShapeDtypeStruct((SHARE, COLS, COLS), BF16),
        ],
        scratch_shapes=[
            pltpu.SMEM((1, 2), jnp.int32),
            pltpu.VMEM((ROWS, COLS), BF16),
            pltpu.SemaphoreType.DMA((3 + 2 * Z,)),
        ],
    )(pair_domain, amplitudes, ov, vv_factors)
    got = lax.all_to_all(sent, "z", 0, 0, tiled=True)
    sent = kernel(spread_kernel, (VIRT * Y, ROWS + PART, COLS), (), (got,))
    near = lax.ppermute(mine, "y", [(y, y ^ 1) for y in range(Y)])
    near = lax.all_gather(near, ("virt", "pair"), axis=0, tiled=True)
    got = lax.all_to_all(sent, ("virt", "y"), 0, 0, tiled=True)
    wide = pltpu.VMEM((COLS, 2 * AUX * COLS), BF16)
    sent = kernel(
        ladder_kernel,
        (VIRT * Y, ROWS + PART, COLS),
        (vv_mask,),
        (got, vv_factors, near),
        (wide, wide),
        40,
    )
    got = lax.all_to_all(sent, ("virt", "y"), 0, 0, tiled=True)
    sent = kernel(sum_kernel, (Z, ROWS + AUX, COLS), (), (got,))
    got = lax.all_to_all(sent, "z", 0, 0, tiled=True)
    return kernel(
        update_kernel,
        (1, 1, ROWS, COLS),
        (pair_domain, occ_energy_i, occ_energy_j),
        (virt_energy[None, :], got, ov),
    )


def solution(mesh):
    fine = Mesh(mesh.devices.reshape(2, VIRT, Y, Z), ("pair", "virt", "y", "z"))
    integ = ("y", "z")
    placed = (
        P("pair", integ, "virt", None),
        P(integ, None, None),
        P(None, integ, None),
        P("pair"),
        P(integ),
        P(),
        P(),
        P("pair", integ, None),
    )
    return jax.shard_map(
        body,
        mesh=fine,
        in_specs=placed,
        out_specs=P("pair", integ, "virt", None),
        check_vma=False,
    )
```

```python
import jax
import jax.numpy as jnp
from jax import lax
from jax.experimental import pallas as pl
from jax.experimental.pallas import tpu as pltpu
from jax.sharding import Mesh
from jax.sharding import PartitionSpec as P

TILE_SIZE = 128
BF16 = jnp.bfloat16
F32 = jnp.float32
NT = (((1,), (1,)), ((), ()))
TN = (((0,), (0,)), ((), ()))
VIRT = 4
Y = 4
Z = 8
ROWS = 64
COLS = 256
AUX = 16
PART = 8
SHARE = 4


def out_kernel(domain_hbm, amp_hbm, ov_hbm, factors_hbm, out_ref, up_ref, down_ref, domain, amp, sems):
    x = lax.axis_index("virt")
    share = lax.axis_index("pair") * SHARE
    copies = [
        pltpu.make_async_copy(domain_hbm.at[0], domain, sems.at[0]),
        pltpu.make_async_copy(amp_hbm.at[0, 0], amp, sems.at[1]),
        pltpu.make_async_copy(factors_hbm.at[pl.ds(share, SHARE)], up_ref, sems.at[2]),
        pltpu.make_async_copy(factors_hbm.at[pl.ds(2 * SHARE + share, SHARE)], down_ref, sems.at[3]),
    ]
    for to in range(Z):
        for high in range(2):
            start = pl.multiple_of(((2 * high + x // 2) * Z + to) * AUX + (x % 2) * PART, PART)
            target = out_ref.at[to, pl.ds(ROWS + high * PART, PART)]
            copies.append(pltpu.make_async_copy(ov_hbm.at[pl.ds(start, PART)], target, sems.at[4 + 2 * to + high]))
    for copy in copies:
        copy.start()
    copies[0].wait()
    copies[1].wait()
    row_tile = domain[0, x // 2]
    for half in range(2):
        cols = slice(half * TILE_SIZE, (half + 1) * TILE_SIZE)
        keep = (row_tile * domain[0, half]).astype(F32)
        rows = (amp[:, cols].astype(F32) * keep).astype(BF16)
        for to in range(Z):
            out_ref[to, :ROWS, cols] = rows
    for copy in copies[2:]:
        copy.wait()


def spread_kernel(got_ref, out_ref):
    for to_x in range(VIRT):
        for to_y in range(Y):
            high, low = divmod(to_y, 2)
            out_ref[to_x * Y + to_y, :ROWS] = got_ref[2 * to_x + low, :ROWS]
            start = ROWS + high * PART
            out_ref[to_x * Y + to_y, ROWS:] = got_ref[2 * to_x + low, start : start + PART]


def ladder_kernel(mask_ref, rows_ref, own_ref, up_ref, down_ref, up2_ref, down2_ref, out_ref, masked, weighted):
    sources = [(own_ref, aux) for aux in range(AUX)]
    sources += [(ref, aux) for ref in (up_ref, down_ref, up2_ref, down2_ref) for aux in range(SHARE)]
    for p in range(2):
        for q in range(2):
            keep = jnp.full((1, TILE_SIZE), mask_ref[p, q], jnp.int32).astype(F32).astype(BF16)
            for slot, (ref, aux) in enumerate(sources):
                block = ref[aux, p * 128 : (p + 1) * 128, q * 128 : (q + 1) * 128] * keep
                masked[p * 128 : (p + 1) * 128, slot * 256 + q * 128 : slot * 256 + (q + 1) * 128] = block

    zeta = jnp.zeros((2 * AUX, COLS), F32)
    for at_y in range(Y):
        amp = jnp.concatenate([rows_ref[at_x * Y + at_y, :ROWS] for at_x in range(VIRT)], axis=0)
        fac = jnp.concatenate([rows_ref[at_x * Y + at_y, ROWS:] for at_x in range(VIRT)], axis=0)
        direct = lax.dot_general(fac, amp, NT, preferred_element_type=F32)
        swapped = jnp.dot(fac, amp, preferred_element_type=F32)
        zeta = zeta + (2.0 * direct - swapped)
        for slot in range(2 * AUX):
            cols = slice(slot * 256, (slot + 1) * 256)
            weighted[:, cols] = jnp.dot(masked[:, cols], amp, preferred_element_type=F32).astype(BF16)
        total = lax.dot_general(weighted[...], masked[...], NT, preferred_element_type=F32).astype(BF16)
        for at_x in range(VIRT):
            out_ref[at_x * Y + at_y, :ROWS] = total[at_x * ROWS : (at_x + 1) * ROWS]
    group = lax.broadcasted_iota(jnp.int32, (PART, COLS), 1) // ROWS
    for at_x in range(VIRT):
        piece = jnp.zeros((PART, COLS), F32)
        for to in range(4):
            turned = zeta[to * PART : (to + 1) * PART]
            if to != at_x:
                turned = pltpu.roll(turned, ((to - at_x) % 4) * ROWS, 1)
            piece = jnp.where(group == to, turned, piece)
        piece = piece.astype(BF16)
        for at_y in range(Y):
            out_ref[at_x * Y + at_y, ROWS:] = piece


def sum_kernel(got_ref, out_ref):
    sums = [jnp.zeros((PART, COLS), F32), jnp.zeros((PART, COLS), F32)]
    for at_x in range(VIRT):
        for low in range(2):
            first = got_ref[at_x * Y + low]
            second = got_ref[at_x * Y + 2 + low]
            out_ref[2 * at_x + low, :ROWS] = (first[:ROWS].astype(F32) + second[:ROWS].astype(F32)).astype(BF16)
            sums[0] = sums[0] + first[ROWS:].astype(F32)
            sums[1] = sums[1] + second[ROWS:].astype(F32)
    group = lax.broadcasted_iota(jnp.int32, (PART, COLS), 1) // ROWS
    halves = []
    for half in range(2):
        piece = jnp.zeros((PART, COLS), F32)
        for high in range(2):
            for low in range(2):
                source, to = 2 * low + half, 2 * high + low
                turned = sums[high]
                if source != to:
                    turned = pltpu.roll(turned, ((to - source) % 4) * ROWS, 1)
                piece = jnp.where(group == to, turned, piece)
        halves.append(piece)
    zeta = jnp.concatenate(halves, axis=0).astype(BF16)
    for to in range(Z):
        out_ref[to, ROWS:] = zeta


def update_kernel(domain_ref, occ_i_ref, occ_j_ref, virt_ref, got_ref, ov_ref, out_ref):
    x = lax.axis_index("virt")
    total = got_ref[0, :ROWS].astype(F32)
    for source in range(1, Z):
        total = total + got_ref[source, :ROWS].astype(F32)
    zeta = got_ref[:, ROWS:].reshape(Z * AUX, COLS)
    for at_y in range(Y):
        part = zeta[:, at_y * ROWS : (at_y + 1) * ROWS]
        fac = ov_ref[at_y * Z * AUX : (at_y + 1) * Z * AUX, :]
        total = total + lax.dot_general(part, fac, TN, preferred_element_type=F32)
    energy = jnp.broadcast_to(virt_ref[...], (ROWS, COLS))
    row = lax.broadcasted_iota(jnp.int32, (ROWS, COLS), 0) + x * ROWS
    lane = lax.broadcasted_iota(jnp.int32, (ROWS, COLS), 1)
    energy_rows = jnp.sum(jnp.where(row == lane, energy, 0.0), axis=1, keepdims=True)
    denom = energy_rows + energy - occ_i_ref[0] - occ_j_ref[0]
    row_tile = domain_ref[0, 0, x // 2]
    left = (row_tile * domain_ref[0, 0, 0]).astype(F32)
    right = (row_tile * domain_ref[0, 0, 1]).astype(F32)
    keep = jnp.where(lane < TILE_SIZE, left, right)
    out_ref[0, 0] = (total * keep / denom).astype(BF16)


def kernel(function, shape, scalars, arrays, scratch=(), mib=16):
    smem = pl.BlockSpec(memory_space=pltpu.SMEM)
    vmem = pl.BlockSpec(memory_space=pltpu.VMEM)
    call = pl.pallas_call(
        function,
        name=function.__name__,
        in_specs=[smem] * len(scalars) + [vmem] * len(arrays),
        out_specs=vmem,
        out_shape=jax.ShapeDtypeStruct(shape, BF16),
        scratch_shapes=list(scratch),
        compiler_params=pltpu.CompilerParams(vmem_limit_bytes=mib << 20),
    )
    return call(*scalars, *arrays)


def body(
    amplitudes,
    vv_factors,
    ov_factors,
    occ_energy_i,
    occ_energy_j,
    virt_energy,
    vv_mask,
    pair_domain,
):
    ov = ov_factors[:, 0, :]
    hbm = pl.BlockSpec(memory_space=pltpu.HBM)
    sent, up, down = pl.pallas_call(
        out_kernel,
        name="out_kernel",
        in_specs=[hbm, hbm, hbm, hbm],
        out_specs=[pl.BlockSpec(memory_space=pltpu.VMEM), hbm, hbm],
        out_shape=[
            jax.ShapeDtypeStruct((Z, ROWS + AUX, COLS), BF16),
            jax.ShapeDtypeStruct((SHARE, COLS, COLS), BF16),
            jax.ShapeDtypeStruct((SHARE, COLS, COLS), BF16),
        ],
        scratch_shapes=[
            pltpu.SMEM((1, 2), jnp.int32),
            pltpu.VMEM((ROWS, COLS), BF16),
            pltpu.SemaphoreType.DMA((4 + 2 * Z,)),
        ],
    )(pair_domain, amplitudes, ov, vv_factors)
    got = lax.all_to_all(sent, "z", 0, 0, tiled=True)
    sent = kernel(spread_kernel, (VIRT * Y, ROWS + PART, COLS), (), (got,))
    swap = [(0, 1), (1, 0)]
    up = lax.ppermute(up, "y", [(y, (y + 1) % Y) for y in range(Y)])
    down = lax.ppermute(down, "y", [(y, (y - 1) % Y) for y in range(Y)])
    extra = (up, down, lax.ppermute(up, "pair", swap), lax.ppermute(down, "pair", swap))
    got = lax.all_to_all(sent, ("virt", "y"), 0, 0, tiled=True)
    wide = pltpu.VMEM((COLS, 2 * AUX * COLS), BF16)
    sent = kernel(
        ladder_kernel,
        (VIRT * Y, ROWS + PART, COLS),
        (vv_mask,),
        (got, vv_factors) + extra,
        (wide, wide),
        40,
    )
    got = lax.all_to_all(sent, ("virt", "y"), 0, 0, tiled=True)
    sent = kernel(sum_kernel, (Z, ROWS + AUX, COLS), (), (got,))
    got = lax.all_to_all(sent, "z", 0, 0, tiled=True)
    return kernel(
        update_kernel,
        (1, 1, ROWS, COLS),
        (pair_domain, occ_energy_i, occ_energy_j),
        (virt_energy[None, :], got, ov),
    )


def solution(mesh):
    fine = Mesh(mesh.devices.reshape(2, VIRT, Y, Z), ("pair", "virt", "y", "z"))
    integ = ("y", "z")
    placed = (
        P("pair", integ, "virt", None),
        P(integ, None, None),
        P(None, integ, None),
        P("pair"),
        P(integ),
        P(),
        P(),
        P("pair", integ, None),
    )
    return jax.shard_map(
        body,
        mesh=fine,
        in_specs=placed,
        out_specs=P("pair", integ, "virt", None),
        check_vma=False,
    )
```

```python
import jax
import jax.numpy as jnp
from jax import lax
from jax.experimental import pallas as pl
from jax.experimental.pallas import tpu as pltpu
from jax.sharding import Mesh
from jax.sharding import PartitionSpec as P

TILE_SIZE = 128
BF16 = jnp.bfloat16
F32 = jnp.float32
NT = (((1,), (1,)), ((), ()))
TN = (((0,), (0,)), ((), ()))
VIRT = 4
Y = 4
Z = 8
ROWS = 64
COLS = 256
AUX = 16
PART = 8
SHARE = 4


def out_kernel(domain_hbm, amp_hbm, ov_hbm, out_ref, domain, amp, sems):
    x = lax.axis_index("virt")
    copies = [
        pltpu.make_async_copy(domain_hbm.at[0], domain, sems.at[0]),
        pltpu.make_async_copy(amp_hbm.at[0, 0], amp, sems.at[1]),
    ]
    for to in range(Z):
        for high in range(2):
            start = pl.multiple_of(((2 * high + x // 2) * Z + to) * AUX + (x % 2) * PART, PART)
            target = out_ref.at[to, pl.ds(ROWS + high * PART, PART)]
            copies.append(pltpu.make_async_copy(ov_hbm.at[pl.ds(start, PART)], target, sems.at[2 + 2 * to + high]))
    for copy in copies:
        copy.start()
    copies[0].wait()
    copies[1].wait()
    row_tile = domain[0, x // 2]
    for half in range(2):
        cols = slice(half * TILE_SIZE, (half + 1) * TILE_SIZE)
        keep = (row_tile * domain[0, half]).astype(F32)
        rows = (amp[:, cols].astype(F32) * keep).astype(BF16)
        for to in range(Z):
            out_ref[to, :ROWS, cols] = rows
    for copy in copies[2:]:
        copy.wait()


def share_kernel(factors_hbm, up_ref, down_ref, sems):
    share = lax.axis_index("pair") * SHARE
    up = pltpu.make_async_copy(factors_hbm.at[pl.ds(share, SHARE)], up_ref, sems.at[0])
    down = pltpu.make_async_copy(factors_hbm.at[pl.ds(2 * SHARE + share, SHARE)], down_ref, sems.at[1])
    up.start()
    down.start()
    up.wait()
    down.wait()


def spread_kernel(got_ref, out_ref):
    for to_x in range(VIRT):
        for to_y in range(Y):
            high, low = divmod(to_y, 2)
            out_ref[to_x * Y + to_y, :ROWS] = got_ref[2 * to_x + low, :ROWS]
            start = ROWS + high * PART
            out_ref[to_x * Y + to_y, ROWS:] = got_ref[2 * to_x + low, start : start + PART]


def ladder_kernel(
    mask_ref, rows_ref, own_hbm, up_hbm, down_hbm, up2_hbm, down2_hbm, out_ref, factors, masked, weighted, sems
):
    sources = [(own_hbm, aux) for aux in range(AUX)]
    sources += [(ref, aux) for ref in (up_hbm, down_hbm, up2_hbm, down2_hbm) for aux in range(SHARE)]
    copies = [
        pltpu.make_async_copy(ref.at[aux], factors.at[slot], sems.at[slot]) for slot, (ref, aux) in enumerate(sources)
    ]
    for copy in copies:
        copy.start()
    keep = [[jnp.full((1, TILE_SIZE), mask_ref[p, q], jnp.int32).astype(F32).astype(BF16) for q in range(2)] for p in range(2)]
    zeta = jnp.zeros((2 * AUX, COLS), F32)
    for at_y in range(Y):
        amp = jnp.concatenate([rows_ref[at_x * Y + at_y, :ROWS] for at_x in range(VIRT)], axis=0)
        fac = jnp.concatenate([rows_ref[at_x * Y + at_y, ROWS:] for at_x in range(VIRT)], axis=0)
        direct = lax.dot_general(fac, amp, NT, preferred_element_type=F32)
        swapped = jnp.dot(fac, amp, preferred_element_type=F32)
        zeta = zeta + (2.0 * direct - swapped)
        for slot in range(2 * AUX):
            cols = slice(slot * COLS, (slot + 1) * COLS)
            if at_y == 0:
                copies[slot].wait()
                for p in range(2):
                    for q in range(2):
                        rows = slice(p * TILE_SIZE, (p + 1) * TILE_SIZE)
                        lanes = slice(q * TILE_SIZE, (q + 1) * TILE_SIZE)
                        left = slot * COLS + q * TILE_SIZE
                        masked[rows, left : left + TILE_SIZE] = factors[slot, rows, lanes] * keep[p][q]
            weighted[:, cols] = jnp.dot(masked[:, cols], amp, preferred_element_type=F32).astype(BF16)
        total = lax.dot_general(weighted[...], masked[...], NT, preferred_element_type=F32).astype(BF16)
        for at_x in range(VIRT):
            out_ref[at_x * Y + at_y, :ROWS] = total[at_x * ROWS : (at_x + 1) * ROWS]
    group = lax.broadcasted_iota(jnp.int32, (PART, COLS), 1) // ROWS
    for at_x in range(VIRT):
        piece = jnp.zeros((PART, COLS), F32)
        for to in range(4):
            turned = zeta[to * PART : (to + 1) * PART]
            if to != at_x:
                turned = pltpu.roll(turned, ((to - at_x) % 4) * ROWS, 1)
            piece = jnp.where(group == to, turned, piece)
        piece = piece.astype(BF16)
        for at_y in range(Y):
            out_ref[at_x * Y + at_y, ROWS:] = piece


def sum_kernel(got_ref, out_ref):
    sums = [jnp.zeros((PART, COLS), F32), jnp.zeros((PART, COLS), F32)]
    for at_x in range(VIRT):
        for low in range(2):
            first = got_ref[at_x * Y + low]
            second = got_ref[at_x * Y + 2 + low]
            out_ref[2 * at_x + low, :ROWS] = (first[:ROWS].astype(F32) + second[:ROWS].astype(F32)).astype(BF16)
            sums[0] = sums[0] + first[ROWS:].astype(F32)
            sums[1] = sums[1] + second[ROWS:].astype(F32)
    group = lax.broadcasted_iota(jnp.int32, (PART, COLS), 1) // ROWS
    halves = []
    for half in range(2):
        piece = jnp.zeros((PART, COLS), F32)
        for high in range(2):
            for low in range(2):
                source, to = 2 * low + half, 2 * high + low
                turned = sums[high]
                if source != to:
                    turned = pltpu.roll(turned, ((to - source) % 4) * ROWS, 1)
                piece = jnp.where(group == to, turned, piece)
        halves.append(piece)
    zeta = jnp.concatenate(halves, axis=0).astype(BF16)
    for to in range(Z):
        out_ref[to, ROWS:] = zeta


def update_kernel(domain_ref, occ_i_ref, occ_j_ref, virt_ref, got_ref, ov_ref, out_ref):
    x = lax.axis_index("virt")
    total = got_ref[0, :ROWS].astype(F32)
    for source in range(1, Z):
        total = total + got_ref[source, :ROWS].astype(F32)
    zeta = got_ref[:, ROWS:].reshape(Z * AUX, COLS)
    for at_y in range(Y):
        part = zeta[:, at_y * ROWS : (at_y + 1) * ROWS]
        fac = ov_ref[at_y * Z * AUX : (at_y + 1) * Z * AUX, :]
        total = total + lax.dot_general(part, fac, TN, preferred_element_type=F32)
    energy = jnp.broadcast_to(virt_ref[...], (ROWS, COLS))
    row = lax.broadcasted_iota(jnp.int32, (ROWS, COLS), 0) + x * ROWS
    lane = lax.broadcasted_iota(jnp.int32, (ROWS, COLS), 1)
    energy_rows = jnp.sum(jnp.where(row == lane, energy, 0.0), axis=1, keepdims=True)
    denom = energy_rows + energy - occ_i_ref[0] - occ_j_ref[0]
    row_tile = domain_ref[0, 0, x // 2]
    left = (row_tile * domain_ref[0, 0, 0]).astype(F32)
    right = (row_tile * domain_ref[0, 0, 1]).astype(F32)
    keep = jnp.where(lane < TILE_SIZE, left, right)
    out_ref[0, 0] = (total * keep / denom).astype(BF16)


def kernel(function, shape, scalars, arrays, scratch=(), mib=16):
    smem = pl.BlockSpec(memory_space=pltpu.SMEM)
    vmem = pl.BlockSpec(memory_space=pltpu.VMEM)
    call = pl.pallas_call(
        function,
        name=function.__name__,
        in_specs=[smem] * len(scalars) + [vmem] * len(arrays),
        out_specs=vmem,
        out_shape=jax.ShapeDtypeStruct(shape, BF16),
        scratch_shapes=list(scratch),
        compiler_params=pltpu.CompilerParams(vmem_limit_bytes=mib << 20),
    )
    return call(*scalars, *arrays)


def body(
    amplitudes,
    vv_factors,
    ov_factors,
    occ_energy_i,
    occ_energy_j,
    virt_energy,
    vv_mask,
    pair_domain,
):
    ov = ov_factors[:, 0, :]
    hbm = pl.BlockSpec(memory_space=pltpu.HBM)
    sent = pl.pallas_call(
        out_kernel,
        name="out_kernel",
        in_specs=[hbm, hbm, hbm],
        out_specs=pl.BlockSpec(memory_space=pltpu.VMEM),
        out_shape=jax.ShapeDtypeStruct((Z, ROWS + AUX, COLS), BF16),
        scratch_shapes=[
            pltpu.SMEM((1, 2), jnp.int32),
            pltpu.VMEM((ROWS, COLS), BF16),
            pltpu.SemaphoreType.DMA((2 + 2 * Z,)),
        ],
    )(pair_domain, amplitudes, ov)
    up, down = pl.pallas_call(
        share_kernel,
        name="share_kernel",
        in_specs=[hbm],
        out_specs=[pl.BlockSpec(memory_space=pltpu.VMEM)] * 2,
        out_shape=[jax.ShapeDtypeStruct((SHARE, COLS, COLS), BF16)] * 2,
        scratch_shapes=[pltpu.SemaphoreType.DMA((2,))],
    )(vv_factors)
    got = lax.all_to_all(sent, "z", 0, 0, tiled=True)
    sent = kernel(spread_kernel, (VIRT * Y, ROWS + PART, COLS), (), (got,))
    swap = [(0, 1), (1, 0)]
    up = lax.ppermute(up, "y", [(y, (y + 1) % Y) for y in range(Y)])
    down = lax.ppermute(down, "y", [(y, (y - 1) % Y) for y in range(Y)])
    extra = (up, down, lax.ppermute(up, "pair", swap), lax.ppermute(down, "pair", swap))
    got = lax.all_to_all(sent, ("virt", "y"), 0, 0, tiled=True)
    wide = pltpu.VMEM((COLS, 2 * AUX * COLS), BF16)
    sent = pl.pallas_call(
        ladder_kernel,
        name="ladder_kernel",
        in_specs=[pl.BlockSpec(memory_space=pltpu.SMEM), pl.BlockSpec(memory_space=pltpu.VMEM)] + [hbm] * 5,
        out_specs=pl.BlockSpec(memory_space=pltpu.VMEM),
        out_shape=jax.ShapeDtypeStruct((VIRT * Y, ROWS + PART, COLS), BF16),
        scratch_shapes=[
            pltpu.VMEM((2 * AUX, COLS, COLS), BF16),
            wide,
            wide,
            pltpu.SemaphoreType.DMA((2 * AUX,)),
        ],
        compiler_params=pltpu.CompilerParams(vmem_limit_bytes=40 << 20),
    )(vv_mask, got, vv_factors, *[pltpu.with_memory_space_constraint(part, pltpu.HBM) for part in extra])
    got = lax.all_to_all(sent, ("virt", "y"), 0, 0, tiled=True)
    sent = kernel(sum_kernel, (Z, ROWS + AUX, COLS), (), (got,))
    got = lax.all_to_all(sent, "z", 0, 0, tiled=True)
    return kernel(
        update_kernel,
        (1, 1, ROWS, COLS),
        (pair_domain, occ_energy_i, occ_energy_j),
        (virt_energy[None, :], got, ov),
    )


def solution(mesh):
    fine = Mesh(mesh.devices.reshape(2, VIRT, Y, Z), ("pair", "virt", "y", "z"))
    integ = ("y", "z")
    placed = (
        P("pair", integ, "virt", None),
        P(integ, None, None),
        P(None, integ, None),
        P("pair"),
        P(integ),
        P(),
        P(),
        P("pair", integ, None),
    )
    return jax.shard_map(
        body,
        mesh=fine,
        in_specs=placed,
        out_specs=P("pair", integ, "virt", None),
        check_vma=False,
    )
```

```python
import jax
import jax.numpy as jnp
from jax import lax
from jax.experimental import pallas as pl
from jax.experimental.pallas import tpu as pltpu
from jax.sharding import Mesh
from jax.sharding import PartitionSpec as P

TILE_SIZE = 128
BF16 = jnp.bfloat16
F32 = jnp.float32
NT = (((1,), (1,)), ((), ()))
TN = (((0,), (0,)), ((), ()))
VIRT = 4
Y = 4
Z = 8
ROWS = 64
COLS = 256
AUX = 16
PART = 8
SHARE = 4


def out_kernel(domain_hbm, amp_hbm, ov_hbm, out_ref, domain, amp, sems):
    x = lax.axis_index("virt")
    copies = [
        pltpu.make_async_copy(domain_hbm.at[0], domain, sems.at[0]),
        pltpu.make_async_copy(amp_hbm.at[0, 0], amp, sems.at[1]),
    ]
    for to in range(Z):
        for high in range(2):
            start = pl.multiple_of(((2 * high + x // 2) * Z + to) * AUX + (x % 2) * PART, PART)
            target = out_ref.at[to, pl.ds(ROWS + high * PART, PART)]
            copies.append(pltpu.make_async_copy(ov_hbm.at[pl.ds(start, PART)], target, sems.at[2 + 2 * to + high]))
    for copy in copies:
        copy.start()
    copies[0].wait()
    copies[1].wait()
    row_tile = domain[0, x // 2]
    for half in range(2):
        cols = slice(half * TILE_SIZE, (half + 1) * TILE_SIZE)
        keep = (row_tile * domain[0, half]).astype(F32)
        rows = (amp[:, cols].astype(F32) * keep).astype(BF16)
        for to in range(Z):
            out_ref[to, :ROWS, cols] = rows
    for copy in copies[2:]:
        copy.wait()


def share_kernel(factors_hbm, up_ref, down_ref, sems):
    share = lax.axis_index("pair") * SHARE
    up = pltpu.make_async_copy(factors_hbm.at[pl.ds(share, SHARE)], up_ref, sems.at[0])
    down = pltpu.make_async_copy(factors_hbm.at[pl.ds(2 * SHARE + share, SHARE)], down_ref, sems.at[1])
    up.start()
    down.start()
    up.wait()
    down.wait()


def spread_kernel(got_ref, out_ref):
    for to_x in range(VIRT):
        for to_y in range(Y):
            high, low = divmod(to_y, 2)
            out_ref[to_x * Y + to_y, :ROWS] = got_ref[2 * to_x + low, :ROWS]
            start = ROWS + high * PART
            out_ref[to_x * Y + to_y, ROWS:] = got_ref[2 * to_x + low, start : start + PART]


def ladder_kernel(
    mask_ref, rows_ref, own_ref, up_hbm, down_hbm, up2_hbm, down2_hbm, out_ref, factors, masked, weighted, sems
):
    copies = [
        pltpu.make_async_copy(ref, factors.at[part], sems.at[part])
        for part, ref in enumerate((up_hbm, down_hbm, up2_hbm, down2_hbm))
    ]
    for copy in copies:
        copy.start()

    def mask(slot, matrix):
        for p in range(2):
            for q in range(2):
                keep = jnp.full((1, TILE_SIZE), mask_ref[p, q], jnp.int32).astype(F32).astype(BF16)
                rows = slice(p * TILE_SIZE, (p + 1) * TILE_SIZE)
                left = slot * COLS + q * TILE_SIZE
                block = matrix[rows, q * TILE_SIZE : (q + 1) * TILE_SIZE]
                masked[rows, left : left + TILE_SIZE] = block * keep

    for aux in range(AUX):
        mask(aux, own_ref.at[aux])
    for part, copy in enumerate(copies):
        copy.wait()
        for aux in range(SHARE):
            mask(AUX + part * SHARE + aux, factors.at[part, aux])

    zeta = jnp.zeros((2 * AUX, COLS), F32)
    for at_y in range(Y):
        amp = jnp.concatenate([rows_ref[at_x * Y + at_y, :ROWS] for at_x in range(VIRT)], axis=0)
        fac = jnp.concatenate([rows_ref[at_x * Y + at_y, ROWS:] for at_x in range(VIRT)], axis=0)
        direct = lax.dot_general(fac, amp, NT, preferred_element_type=F32)
        swapped = jnp.dot(fac, amp, preferred_element_type=F32)
        zeta = zeta + (2.0 * direct - swapped)
        for slot in range(2 * AUX):
            cols = slice(slot * COLS, (slot + 1) * COLS)
            weighted[:, cols] = jnp.dot(masked[:, cols], amp, preferred_element_type=F32).astype(BF16)
        total = lax.dot_general(weighted[...], masked[...], NT, preferred_element_type=F32).astype(BF16)
        for at_x in range(VIRT):
            out_ref[at_x * Y + at_y, :ROWS] = total[at_x * ROWS : (at_x + 1) * ROWS]
    group = lax.broadcasted_iota(jnp.int32, (PART, COLS), 1) // ROWS
    for at_x in range(VIRT):
        piece = jnp.zeros((PART, COLS), F32)
        for to in range(4):
            turned = zeta[to * PART : (to + 1) * PART]
            if to != at_x:
                turned = pltpu.roll(turned, ((to - at_x) % 4) * ROWS, 1)
            piece = jnp.where(group == to, turned, piece)
        piece = piece.astype(BF16)
        for at_y in range(Y):
            out_ref[at_x * Y + at_y, ROWS:] = piece


def sum_kernel(got_ref, out_ref):
    sums = [jnp.zeros((PART, COLS), F32), jnp.zeros((PART, COLS), F32)]
    for at_x in range(VIRT):
        for low in range(2):
            first = got_ref[at_x * Y + low]
            second = got_ref[at_x * Y + 2 + low]
            out_ref[2 * at_x + low, :ROWS] = (first[:ROWS].astype(F32) + second[:ROWS].astype(F32)).astype(BF16)
            sums[0] = sums[0] + first[ROWS:].astype(F32)
            sums[1] = sums[1] + second[ROWS:].astype(F32)
    group = lax.broadcasted_iota(jnp.int32, (PART, COLS), 1) // ROWS
    halves = []
    for half in range(2):
        piece = jnp.zeros((PART, COLS), F32)
        for high in range(2):
            for low in range(2):
                source, to = 2 * low + half, 2 * high + low
                turned = sums[high]
                if source != to:
                    turned = pltpu.roll(turned, ((to - source) % 4) * ROWS, 1)
                piece = jnp.where(group == to, turned, piece)
        halves.append(piece)
    zeta = jnp.concatenate(halves, axis=0).astype(BF16)
    for to in range(Z):
        out_ref[to, ROWS:] = zeta


def update_kernel(domain_ref, occ_i_ref, occ_j_ref, virt_ref, got_ref, ov_ref, out_ref):
    x = lax.axis_index("virt")
    total = got_ref[0, :ROWS].astype(F32)
    for source in range(1, Z):
        total = total + got_ref[source, :ROWS].astype(F32)
    zeta = got_ref[:, ROWS:].reshape(Z * AUX, COLS)
    for at_y in range(Y):
        part = zeta[:, at_y * ROWS : (at_y + 1) * ROWS]
        fac = ov_ref[at_y * Z * AUX : (at_y + 1) * Z * AUX, :]
        total = total + lax.dot_general(part, fac, TN, preferred_element_type=F32)
    energy = jnp.broadcast_to(virt_ref[...], (ROWS, COLS))
    row = lax.broadcasted_iota(jnp.int32, (ROWS, COLS), 0) + x * ROWS
    lane = lax.broadcasted_iota(jnp.int32, (ROWS, COLS), 1)
    energy_rows = jnp.sum(jnp.where(row == lane, energy, 0.0), axis=1, keepdims=True)
    denom = energy_rows + energy - occ_i_ref[0] - occ_j_ref[0]
    row_tile = domain_ref[0, 0, x // 2]
    left = (row_tile * domain_ref[0, 0, 0]).astype(F32)
    right = (row_tile * domain_ref[0, 0, 1]).astype(F32)
    keep = jnp.where(lane < TILE_SIZE, left, right)
    out_ref[0, 0] = (total * keep / denom).astype(BF16)


def kernel(function, shape, scalars, arrays, scratch=(), mib=16):
    smem = pl.BlockSpec(memory_space=pltpu.SMEM)
    vmem = pl.BlockSpec(memory_space=pltpu.VMEM)
    call = pl.pallas_call(
        function,
        name=function.__name__,
        in_specs=[smem] * len(scalars) + [vmem] * len(arrays),
        out_specs=vmem,
        out_shape=jax.ShapeDtypeStruct(shape, BF16),
        scratch_shapes=list(scratch),
        compiler_params=pltpu.CompilerParams(vmem_limit_bytes=mib << 20),
    )
    return call(*scalars, *arrays)


def body(
    amplitudes,
    vv_factors,
    ov_factors,
    occ_energy_i,
    occ_energy_j,
    virt_energy,
    vv_mask,
    pair_domain,
):
    ov = ov_factors[:, 0, :]
    hbm = pl.BlockSpec(memory_space=pltpu.HBM)
    sent = pl.pallas_call(
        out_kernel,
        name="out_kernel",
        in_specs=[hbm, hbm, hbm],
        out_specs=pl.BlockSpec(memory_space=pltpu.VMEM),
        out_shape=jax.ShapeDtypeStruct((Z, ROWS + AUX, COLS), BF16),
        scratch_shapes=[
            pltpu.SMEM((1, 2), jnp.int32),
            pltpu.VMEM((ROWS, COLS), BF16),
            pltpu.SemaphoreType.DMA((2 + 2 * Z,)),
        ],
    )(pair_domain, amplitudes, ov)
    up, down = pl.pallas_call(
        share_kernel,
        name="share_kernel",
        in_specs=[hbm],
        out_specs=[pl.BlockSpec(memory_space=pltpu.VMEM)] * 2,
        out_shape=[jax.ShapeDtypeStruct((SHARE, COLS, COLS), BF16)] * 2,
        scratch_shapes=[pltpu.SemaphoreType.DMA((2,))],
    )(vv_factors)
    got = lax.all_to_all(sent, "z", 0, 0, tiled=True)
    sent = kernel(spread_kernel, (VIRT * Y, ROWS + PART, COLS), (), (got,))
    swap = [(0, 1), (1, 0)]
    up = lax.ppermute(up, "y", [(y, (y + 1) % Y) for y in range(Y)])
    down = lax.ppermute(down, "y", [(y, (y - 1) % Y) for y in range(Y)])
    extra = (up, down, lax.ppermute(up, "pair", swap), lax.ppermute(down, "pair", swap))
    got = lax.all_to_all(sent, ("virt", "y"), 0, 0, tiled=True)
    wide = pltpu.VMEM((COLS, 2 * AUX * COLS), BF16)
    sent = pl.pallas_call(
        ladder_kernel,
        name="ladder_kernel",
        in_specs=[pl.BlockSpec(memory_space=pltpu.SMEM)] + [pl.BlockSpec(memory_space=pltpu.VMEM)] * 2 + [hbm] * 4,
        out_specs=pl.BlockSpec(memory_space=pltpu.VMEM),
        out_shape=jax.ShapeDtypeStruct((VIRT * Y, ROWS + PART, COLS), BF16),
        scratch_shapes=[
            pltpu.VMEM((4, SHARE, COLS, COLS), BF16),
            wide,
            wide,
            pltpu.SemaphoreType.DMA((4,)),
        ],
        compiler_params=pltpu.CompilerParams(vmem_limit_bytes=40 << 20),
    )(vv_mask, got, vv_factors, *[pltpu.with_memory_space_constraint(part, pltpu.HBM) for part in extra])
    got = lax.all_to_all(sent, ("virt", "y"), 0, 0, tiled=True)
    sent = kernel(sum_kernel, (Z, ROWS + AUX, COLS), (), (got,))
    got = lax.all_to_all(sent, "z", 0, 0, tiled=True)
    return kernel(
        update_kernel,
        (1, 1, ROWS, COLS),
        (pair_domain, occ_energy_i, occ_energy_j),
        (virt_energy[None, :], got, ov),
    )


def solution(mesh):
    fine = Mesh(mesh.devices.reshape(2, VIRT, Y, Z), ("pair", "virt", "y", "z"))
    integ = ("y", "z")
    placed = (
        P("pair", integ, "virt", None),
        P(integ, None, None),
        P(None, integ, None),
        P("pair"),
        P(integ),
        P(),
        P(),
        P("pair", integ, None),
    )
    return jax.shard_map(
        body,
        mesh=fine,
        in_specs=placed,
        out_specs=P("pair", integ, "virt", None),
        check_vma=False,
    )
```

```python
import jax
import jax.numpy as jnp
from jax import lax
from jax.experimental import pallas as pl
from jax.experimental.pallas import tpu as pltpu
from jax.sharding import Mesh
from jax.sharding import PartitionSpec as P

TILE_SIZE = 128
BF16 = jnp.bfloat16
F32 = jnp.float32
NT = (((1,), (1,)), ((), ()))
TN = (((0,), (0,)), ((), ()))
VIRT = 4
Y = 4
Z = 8
ROWS = 64
COLS = 256
AUX = 16
PART = 8
SHARE = 4


def out_kernel(domain_hbm, amp_hbm, ov_hbm, out_ref, domain, amp, sems):
    x = lax.axis_index("virt")
    copies = [
        pltpu.make_async_copy(domain_hbm.at[0], domain, sems.at[0]),
        pltpu.make_async_copy(amp_hbm.at[0, 0], amp, sems.at[1]),
    ]
    for to in range(Z):
        for high in range(2):
            start = pl.multiple_of(((2 * high + x // 2) * Z + to) * AUX + (x % 2) * PART, PART)
            target = out_ref.at[to, pl.ds(ROWS + high * PART, PART)]
            copies.append(pltpu.make_async_copy(ov_hbm.at[pl.ds(start, PART)], target, sems.at[2 + 2 * to + high]))
    for copy in copies:
        copy.start()
    copies[0].wait()
    copies[1].wait()
    row_tile = domain[0, x // 2]
    for half in range(2):
        cols = slice(half * TILE_SIZE, (half + 1) * TILE_SIZE)
        keep = (row_tile * domain[0, half]).astype(F32)
        rows = (amp[:, cols].astype(F32) * keep).astype(BF16)
        for to in range(Z):
            out_ref[to, :ROWS, cols] = rows
    for copy in copies[2:]:
        copy.wait()


def share_kernel(factors_hbm, up_ref, down_ref, sems):
    share = lax.axis_index("pair") * SHARE
    up = pltpu.make_async_copy(factors_hbm.at[pl.ds(share, SHARE)], up_ref, sems.at[0])
    down = pltpu.make_async_copy(factors_hbm.at[pl.ds(2 * SHARE + share, SHARE)], down_ref, sems.at[1])
    up.start()
    down.start()
    up.wait()
    down.wait()


def spread_kernel(got_ref, out_ref):
    for to_x in range(VIRT):
        for to_y in range(Y):
            high, low = divmod(to_y, 2)
            out_ref[to_x * Y + to_y, :ROWS] = got_ref[2 * to_x + low, :ROWS]
            start = ROWS + high * PART
            out_ref[to_x * Y + to_y, ROWS:] = got_ref[2 * to_x + low, start : start + PART]


def mask_kernel(mask_ref, *refs):
    out_ref = refs[-1]
    sources = [(ref, aux) for ref in refs[:-1] for aux in range(ref.shape[0])]
    for p in range(2):
        rows = slice(p * TILE_SIZE, (p + 1) * TILE_SIZE)
        for q in range(2):
            keep = jnp.full((1, TILE_SIZE), mask_ref[p, q], jnp.int32).astype(F32).astype(BF16)
            for slot, (ref, aux) in enumerate(sources):
                left = slot * COLS + q * TILE_SIZE
                block = ref[aux, rows, q * TILE_SIZE : (q + 1) * TILE_SIZE]
                out_ref[rows, left : left + TILE_SIZE] = block * keep


def ladder_kernel(mask_ref, rows_ref, own_ref, extra_hbm, out_ref, own, extra, weighted, sem):
    copy = pltpu.make_async_copy(extra_hbm, extra, sem)
    copy.start()
    mask_kernel(mask_ref, own_ref, own)
    zeta = jnp.zeros((2 * AUX, COLS), F32)
    for at_y in range(Y):
        amp = jnp.concatenate([rows_ref[at_x * Y + at_y, :ROWS] for at_x in range(VIRT)], axis=0)
        fac = jnp.concatenate([rows_ref[at_x * Y + at_y, ROWS:] for at_x in range(VIRT)], axis=0)
        direct = lax.dot_general(fac, amp, NT, preferred_element_type=F32)
        swapped = jnp.dot(fac, amp, preferred_element_type=F32)
        zeta = zeta + (2.0 * direct - swapped)
        total = jnp.zeros((COLS, COLS), F32)
        for half, masked in enumerate((own, extra)):
            if at_y == 0 and half == 1:
                copy.wait()
            for slot in range(AUX):
                cols = slice(slot * COLS, (slot + 1) * COLS)
                piece = jnp.dot(masked[:, cols], amp, preferred_element_type=F32).astype(BF16)
                weighted[half, :, cols] = piece
            total = total + lax.dot_general(weighted[half], masked[...], NT, preferred_element_type=F32)
        total = total.astype(BF16)
        for at_x in range(VIRT):
            out_ref[at_x * Y + at_y, :ROWS] = total[at_x * ROWS : (at_x + 1) * ROWS]
    group = lax.broadcasted_iota(jnp.int32, (PART, COLS), 1) // ROWS
    for at_x in range(VIRT):
        piece = jnp.zeros((PART, COLS), F32)
        for to in range(4):
            turned = zeta[to * PART : (to + 1) * PART]
            if to != at_x:
                turned = pltpu.roll(turned, ((to - at_x) % 4) * ROWS, 1)
            piece = jnp.where(group == to, turned, piece)
        piece = piece.astype(BF16)
        for at_y in range(Y):
            out_ref[at_x * Y + at_y, ROWS:] = piece


def sum_kernel(got_ref, out_ref):
    sums = [jnp.zeros((PART, COLS), F32), jnp.zeros((PART, COLS), F32)]
    for at_x in range(VIRT):
        for low in range(2):
            first = got_ref[at_x * Y + low]
            second = got_ref[at_x * Y + 2 + low]
            out_ref[2 * at_x + low, :ROWS] = (first[:ROWS].astype(F32) + second[:ROWS].astype(F32)).astype(BF16)
            sums[0] = sums[0] + first[ROWS:].astype(F32)
            sums[1] = sums[1] + second[ROWS:].astype(F32)
    group = lax.broadcasted_iota(jnp.int32, (PART, COLS), 1) // ROWS
    halves = []
    for half in range(2):
        piece = jnp.zeros((PART, COLS), F32)
        for high in range(2):
            for low in range(2):
                source, to = 2 * low + half, 2 * high + low
                turned = sums[high]
                if source != to:
                    turned = pltpu.roll(turned, ((to - source) % 4) * ROWS, 1)
                piece = jnp.where(group == to, turned, piece)
        halves.append(piece)
    zeta = jnp.concatenate(halves, axis=0).astype(BF16)
    for to in range(Z):
        out_ref[to, ROWS:] = zeta


def scale_kernel(domain_ref, occ_i_ref, occ_j_ref, virt_ref, out_ref):
    x = lax.axis_index("virt")
    energy = jnp.broadcast_to(virt_ref[...], (ROWS, COLS))
    row = lax.broadcasted_iota(jnp.int32, (ROWS, COLS), 0) + x * ROWS
    lane = lax.broadcasted_iota(jnp.int32, (ROWS, COLS), 1)
    energy_rows = jnp.sum(jnp.where(row == lane, energy, 0.0), axis=1, keepdims=True)
    denom = energy_rows + energy - occ_i_ref[0] - occ_j_ref[0]
    row_tile = domain_ref[0, 0, x // 2]
    left = (row_tile * domain_ref[0, 0, 0]).astype(F32)
    right = (row_tile * domain_ref[0, 0, 1]).astype(F32)
    out_ref[...] = jnp.where(lane < TILE_SIZE, left, right) / denom


def update_kernel(got_ref, ov_ref, scale_ref, out_ref):
    total = got_ref[0, :ROWS].astype(F32)
    for source in range(1, Z):
        total = total + got_ref[source, :ROWS].astype(F32)
    zeta = got_ref[:, ROWS:].reshape(Z * AUX, COLS)
    for at_y in range(Y):
        part = zeta[:, at_y * ROWS : (at_y + 1) * ROWS]
        fac = ov_ref[at_y * Z * AUX : (at_y + 1) * Z * AUX, :]
        total = total + lax.dot_general(part, fac, TN, preferred_element_type=F32)
    out_ref[0, 0] = (total * scale_ref[...]).astype(BF16)


def kernel(function, shape, scalars, arrays, scratch=(), mib=16, dtype=BF16):
    smem = pl.BlockSpec(memory_space=pltpu.SMEM)
    vmem = pl.BlockSpec(memory_space=pltpu.VMEM)
    call = pl.pallas_call(
        function,
        name=function.__name__,
        in_specs=[smem] * len(scalars) + [vmem] * len(arrays),
        out_specs=vmem,
        out_shape=jax.ShapeDtypeStruct(shape, dtype),
        scratch_shapes=list(scratch),
        compiler_params=pltpu.CompilerParams(vmem_limit_bytes=mib << 20),
    )
    return call(*scalars, *arrays)


def body(
    amplitudes,
    vv_factors,
    ov_factors,
    occ_energy_i,
    occ_energy_j,
    virt_energy,
    vv_mask,
    pair_domain,
):
    ov = ov_factors[:, 0, :]
    hbm = pl.BlockSpec(memory_space=pltpu.HBM)
    sent = pl.pallas_call(
        out_kernel,
        name="out_kernel",
        in_specs=[hbm, hbm, hbm],
        out_specs=pl.BlockSpec(memory_space=pltpu.VMEM),
        out_shape=jax.ShapeDtypeStruct((Z, ROWS + AUX, COLS), BF16),
        scratch_shapes=[
            pltpu.SMEM((1, 2), jnp.int32),
            pltpu.VMEM((ROWS, COLS), BF16),
            pltpu.SemaphoreType.DMA((2 + 2 * Z,)),
        ],
    )(pair_domain, amplitudes, ov)
    up, down = pl.pallas_call(
        share_kernel,
        name="share_kernel",
        in_specs=[hbm],
        out_specs=[pl.BlockSpec(memory_space=pltpu.VMEM)] * 2,
        out_shape=[jax.ShapeDtypeStruct((SHARE, COLS, COLS), BF16)] * 2,
        scratch_shapes=[pltpu.SemaphoreType.DMA((2,))],
    )(vv_factors)
    got = lax.all_to_all(sent, "z", 0, 0, tiled=True)
    sent = kernel(spread_kernel, (VIRT * Y, ROWS + PART, COLS), (), (got,))
    swap = [(0, 1), (1, 0)]
    up = lax.ppermute(up, "y", [(y, (y + 1) % Y) for y in range(Y)])
    down = lax.ppermute(down, "y", [(y, (y - 1) % Y) for y in range(Y)])
    extra = (up, down, lax.ppermute(up, "pair", swap), lax.ppermute(down, "pair", swap))
    got = lax.all_to_all(sent, ("virt", "y"), 0, 0, tiled=True)
    packed = (COLS, AUX * COLS)
    extra = kernel(mask_kernel, packed, (vv_mask,), extra)
    smem, vmem = pl.BlockSpec(memory_space=pltpu.SMEM), pl.BlockSpec(memory_space=pltpu.VMEM)
    sent = pl.pallas_call(
        ladder_kernel,
        name="ladder_kernel",
        in_specs=[smem, vmem, vmem, hbm],
        out_specs=vmem,
        out_shape=jax.ShapeDtypeStruct((VIRT * Y, ROWS + PART, COLS), BF16),
        scratch_shapes=[
            pltpu.VMEM(packed, BF16),
            pltpu.VMEM(packed, BF16),
            pltpu.VMEM((2,) + packed, BF16),
            pltpu.SemaphoreType.DMA,
        ],
        compiler_params=pltpu.CompilerParams(vmem_limit_bytes=40 << 20),
    )(vv_mask, got, vv_factors, pltpu.with_memory_space_constraint(extra, pltpu.HBM))
    got = lax.all_to_all(sent, ("virt", "y"), 0, 0, tiled=True)
    sent = kernel(sum_kernel, (Z, ROWS + AUX, COLS), (), (got,))
    got = lax.all_to_all(sent, "z", 0, 0, tiled=True)
    scalars = (pair_domain, occ_energy_i, occ_energy_j)
    scale = kernel(scale_kernel, (ROWS, COLS), scalars, (virt_energy[None, :],), dtype=F32)
    return kernel(update_kernel, (1, 1, ROWS, COLS), (), (got, ov, scale))


def solution(mesh):
    fine = Mesh(mesh.devices.reshape(2, VIRT, Y, Z), ("pair", "virt", "y", "z"))
    integ = ("y", "z")
    placed = (
        P("pair", integ, "virt", None),
        P(integ, None, None),
        P(None, integ, None),
        P("pair"),
        P(integ),
        P(),
        P(),
        P("pair", integ, None),
    )
    return jax.shard_map(
        body,
        mesh=fine,
        in_specs=placed,
        out_specs=P("pair", integ, "virt", None),
        check_vma=False,
    )
```

```python
import jax
import jax.numpy as jnp
from jax import lax
from jax.experimental import pallas as pl
from jax.experimental.pallas import tpu as pltpu
from jax.sharding import Mesh
from jax.sharding import PartitionSpec as P

TILE_SIZE = 128
BF16 = jnp.bfloat16
F32 = jnp.float32
NT = (((1,), (1,)), ((), ()))
TN = (((0,), (0,)), ((), ()))
VIRT = 4
Y = 4
Z = 8
ROWS = 64
COLS = 256
AUX = 16
PART = 8
SHARE = 4


def out_kernel(domain_hbm, amp_hbm, ov_hbm, out_ref, domain, amp, sems):
    x = lax.axis_index("virt")
    copies = [
        pltpu.make_async_copy(domain_hbm.at[0], domain, sems.at[0]),
        pltpu.make_async_copy(amp_hbm.at[0, 0], amp, sems.at[1]),
    ]
    for to in range(Z):
        for high in range(2):
            start = pl.multiple_of(((2 * high + x // 2) * Z + to) * AUX + (x % 2) * PART, PART)
            target = out_ref.at[to, pl.ds(ROWS + high * PART, PART)]
            copies.append(pltpu.make_async_copy(ov_hbm.at[pl.ds(start, PART)], target, sems.at[2 + 2 * to + high]))
    for copy in copies:
        copy.start()
    copies[0].wait()
    copies[1].wait()
    row_tile = domain[0, x // 2]
    for half in range(2):
        cols = slice(half * TILE_SIZE, (half + 1) * TILE_SIZE)
        keep = (row_tile * domain[0, half]).astype(F32)
        rows = (amp[:, cols].astype(F32) * keep).astype(BF16)
        for to in range(Z):
            out_ref[to, :ROWS, cols] = rows
    for copy in copies[2:]:
        copy.wait()


def share_kernel(factors_hbm, up_ref, down_ref, sems):
    share = lax.axis_index("pair") * SHARE
    up = pltpu.make_async_copy(factors_hbm.at[pl.ds(share, SHARE)], up_ref, sems.at[0])
    down = pltpu.make_async_copy(factors_hbm.at[pl.ds(2 * SHARE + share, SHARE)], down_ref, sems.at[1])
    up.start()
    down.start()
    up.wait()
    down.wait()


def spread_kernel(got_ref, out_ref):
    for to_x in range(VIRT):
        for to_y in range(Y):
            high, low = divmod(to_y, 2)
            out_ref[to_x * Y + to_y, :ROWS] = got_ref[2 * to_x + low, :ROWS]
            start = ROWS + high * PART
            out_ref[to_x * Y + to_y, ROWS:] = got_ref[2 * to_x + low, start : start + PART]


def mask_into(masked, slot, matrix, mask_ref):
    for p in range(2):
        for q in range(2):
            keep = jnp.full((1, TILE_SIZE), mask_ref[p, q], jnp.int32).astype(F32).astype(BF16)
            rows = slice(p * TILE_SIZE, (p + 1) * TILE_SIZE)
            left = slot * COLS + q * TILE_SIZE
            block = matrix[rows, q * TILE_SIZE : (q + 1) * TILE_SIZE]
            masked[rows, left : left + TILE_SIZE] = block * keep


def gather_rows(rows_ref, at_y, rows):
    return jnp.concatenate([rows_ref[at_x * Y + at_y, rows] for at_x in range(VIRT)], axis=0)


def ladder_sum(masked, weighted, amp):
    for slot in range(masked.shape[1] // COLS):
        cols = slice(slot * COLS, (slot + 1) * COLS)
        weighted[:, cols] = jnp.dot(masked[:, cols], amp, preferred_element_type=F32).astype(BF16)
    return lax.dot_general(weighted[...], masked[...], NT, preferred_element_type=F32)


def first_kernel(mask_ref, rows_ref, own_ref, up_hbm, down_hbm, sums_ref, zeta_ref, factors, masked, weighted, sems):
    copies = [
        pltpu.make_async_copy(ref, factors.at[part], sems.at[part]) for part, ref in enumerate((up_hbm, down_hbm))
    ]
    for copy in copies:
        copy.start()
    for aux in range(AUX):
        mask_into(masked, aux, own_ref.at[aux], mask_ref)
    for part, copy in enumerate(copies):
        copy.wait()
        for aux in range(SHARE):
            mask_into(masked, AUX + part * SHARE + aux, factors.at[part, aux], mask_ref)
    zeta = jnp.zeros((2 * AUX, COLS), F32)
    for at_y in range(Y):
        amp = gather_rows(rows_ref, at_y, slice(0, ROWS))
        fac = gather_rows(rows_ref, at_y, slice(ROWS, ROWS + PART))
        direct = lax.dot_general(fac, amp, NT, preferred_element_type=F32)
        swapped = jnp.dot(fac, amp, preferred_element_type=F32)
        zeta = zeta + (2.0 * direct - swapped)
        sums_ref[at_y] = ladder_sum(masked, weighted, amp)
    zeta_ref[...] = zeta


def second_kernel(mask_ref, rows_ref, zeta_ref, sums_ref, up_hbm, down_hbm, out_ref, factors, masked, weighted, sems):
    copies = [
        pltpu.make_async_copy(ref, factors.at[part], sems.at[part]) for part, ref in enumerate((up_hbm, down_hbm))
    ]
    for copy in copies:
        copy.start()
    zeta = zeta_ref[...]
    group = lax.broadcasted_iota(jnp.int32, (PART, COLS), 1) // ROWS
    for at_x in range(VIRT):
        piece = jnp.zeros((PART, COLS), F32)
        for to in range(4):
            turned = zeta[to * PART : (to + 1) * PART]
            if to != at_x:
                turned = pltpu.roll(turned, ((to - at_x) % 4) * ROWS, 1)
            piece = jnp.where(group == to, turned, piece)
        piece = piece.astype(BF16)
        for at_y in range(Y):
            out_ref[at_x * Y + at_y, ROWS:] = piece
    for part in range(2):
        copies[part].wait()
        for aux in range(SHARE):
            mask_into(masked, part * SHARE + aux, factors.at[part, aux], mask_ref)
    for at_y in range(Y):
        amp = gather_rows(rows_ref, at_y, slice(0, ROWS))
        total = (sums_ref[at_y] + ladder_sum(masked, weighted, amp)).astype(BF16)
        for at_x in range(VIRT):
            out_ref[at_x * Y + at_y, :ROWS] = total[at_x * ROWS : (at_x + 1) * ROWS]


def sum_kernel(got_ref, out_ref):
    sums = [jnp.zeros((PART, COLS), F32), jnp.zeros((PART, COLS), F32)]
    for at_x in range(VIRT):
        for low in range(2):
            first = got_ref[at_x * Y + low]
            second = got_ref[at_x * Y + 2 + low]
            out_ref[2 * at_x + low, :ROWS] = (first[:ROWS].astype(F32) + second[:ROWS].astype(F32)).astype(BF16)
            sums[0] = sums[0] + first[ROWS:].astype(F32)
            sums[1] = sums[1] + second[ROWS:].astype(F32)
    group = lax.broadcasted_iota(jnp.int32, (PART, COLS), 1) // ROWS
    halves = []
    for half in range(2):
        piece = jnp.zeros((PART, COLS), F32)
        for high in range(2):
            for low in range(2):
                source, to = 2 * low + half, 2 * high + low
                turned = sums[high]
                if source != to:
                    turned = pltpu.roll(turned, ((to - source) % 4) * ROWS, 1)
                piece = jnp.where(group == to, turned, piece)
        halves.append(piece)
    zeta = jnp.concatenate(halves, axis=0).astype(BF16)
    for to in range(Z):
        out_ref[to, ROWS:] = zeta


def scale_kernel(domain_ref, occ_i_ref, occ_j_ref, virt_ref, out_ref):
    x = lax.axis_index("virt")
    energy = jnp.broadcast_to(virt_ref[...], (ROWS, COLS))
    row = lax.broadcasted_iota(jnp.int32, (ROWS, COLS), 0) + x * ROWS
    lane = lax.broadcasted_iota(jnp.int32, (ROWS, COLS), 1)
    energy_rows = jnp.sum(jnp.where(row == lane, energy, 0.0), axis=1, keepdims=True)
    denom = energy_rows + energy - occ_i_ref[0] - occ_j_ref[0]
    row_tile = domain_ref[0, 0, x // 2]
    left = (row_tile * domain_ref[0, 0, 0]).astype(F32)
    right = (row_tile * domain_ref[0, 0, 1]).astype(F32)
    out_ref[...] = jnp.where(lane < TILE_SIZE, left, right) / denom


def update_kernel(got_ref, ov_ref, scale_ref, out_ref):
    total = got_ref[0, :ROWS].astype(F32)
    for source in range(1, Z):
        total = total + got_ref[source, :ROWS].astype(F32)
    zeta = got_ref[:, ROWS:].reshape(Z * AUX, COLS)
    for at_y in range(Y):
        part = zeta[:, at_y * ROWS : (at_y + 1) * ROWS]
        fac = ov_ref[at_y * Z * AUX : (at_y + 1) * Z * AUX, :]
        total = total + lax.dot_general(part, fac, TN, preferred_element_type=F32)
    out_ref[0, 0] = (total * scale_ref[...]).astype(BF16)


def in_hbm(array):
    return pltpu.with_memory_space_constraint(array, pltpu.HBM)


def kernel(function, shape, scalars, arrays, scratch=(), mib=16, dtype=BF16):
    smem = pl.BlockSpec(memory_space=pltpu.SMEM)
    vmem = pl.BlockSpec(memory_space=pltpu.VMEM)
    call = pl.pallas_call(
        function,
        name=function.__name__,
        in_specs=[smem] * len(scalars) + [vmem] * len(arrays),
        out_specs=vmem,
        out_shape=jax.ShapeDtypeStruct(shape, dtype),
        scratch_shapes=list(scratch),
        compiler_params=pltpu.CompilerParams(vmem_limit_bytes=mib << 20),
    )
    return call(*scalars, *arrays)


def body(
    amplitudes,
    vv_factors,
    ov_factors,
    occ_energy_i,
    occ_energy_j,
    virt_energy,
    vv_mask,
    pair_domain,
):
    ov = ov_factors[:, 0, :]
    hbm = pl.BlockSpec(memory_space=pltpu.HBM)
    sent = pl.pallas_call(
        out_kernel,
        name="out_kernel",
        in_specs=[hbm, hbm, hbm],
        out_specs=pl.BlockSpec(memory_space=pltpu.VMEM),
        out_shape=jax.ShapeDtypeStruct((Z, ROWS + AUX, COLS), BF16),
        scratch_shapes=[
            pltpu.SMEM((1, 2), jnp.int32),
            pltpu.VMEM((ROWS, COLS), BF16),
            pltpu.SemaphoreType.DMA((2 + 2 * Z,)),
        ],
    )(pair_domain, amplitudes, ov)
    up, down = pl.pallas_call(
        share_kernel,
        name="share_kernel",
        in_specs=[hbm],
        out_specs=[pl.BlockSpec(memory_space=pltpu.VMEM)] * 2,
        out_shape=[jax.ShapeDtypeStruct((SHARE, COLS, COLS), BF16)] * 2,
        scratch_shapes=[pltpu.SemaphoreType.DMA((2,))],
    )(vv_factors)
    got = lax.all_to_all(sent, "z", 0, 0, tiled=True)
    sent = kernel(spread_kernel, (VIRT * Y, ROWS + PART, COLS), (), (got,))
    swap = [(0, 1), (1, 0)]
    up = lax.ppermute(up, "y", [(y, (y + 1) % Y) for y in range(Y)])
    down = lax.ppermute(down, "y", [(y, (y - 1) % Y) for y in range(Y)])
    got = lax.all_to_all(sent, ("virt", "y"), 0, 0, tiled=True)
    up2 = lax.ppermute(up, "pair", swap)
    down2 = lax.ppermute(down, "pair", swap)
    smem, vmem = pl.BlockSpec(memory_space=pltpu.SMEM), pl.BlockSpec(memory_space=pltpu.VMEM)
    shares = pltpu.VMEM((2, SHARE, COLS, COLS), BF16)
    all_sums = (Y, COLS, COLS)
    sums, zeta = pl.pallas_call(
        first_kernel,
        name="first_kernel",
        in_specs=[smem, vmem, vmem, hbm, hbm],
        out_specs=[vmem, vmem],
        out_shape=[jax.ShapeDtypeStruct(all_sums, F32), jax.ShapeDtypeStruct((2 * AUX, COLS), F32)],
        scratch_shapes=[
            shares,
            pltpu.VMEM((COLS, 3 * PART * COLS), BF16),
            pltpu.VMEM((COLS, 3 * PART * COLS), BF16),
            pltpu.SemaphoreType.DMA((2,)),
        ],
        compiler_params=pltpu.CompilerParams(vmem_limit_bytes=32 << 20),
    )(vv_mask, got, vv_factors, in_hbm(up), in_hbm(down))
    sent = pl.pallas_call(
        second_kernel,
        name="second_kernel",
        in_specs=[smem, vmem, vmem, vmem, hbm, hbm],
        out_specs=vmem,
        out_shape=jax.ShapeDtypeStruct((VIRT * Y, ROWS + PART, COLS), BF16),
        scratch_shapes=[
            shares,
            pltpu.VMEM((COLS, PART * COLS), BF16),
            pltpu.VMEM((COLS, PART * COLS), BF16),
            pltpu.SemaphoreType.DMA((2,)),
        ],
        compiler_params=pltpu.CompilerParams(vmem_limit_bytes=32 << 20),
    )(vv_mask, got, zeta, sums, in_hbm(up2), in_hbm(down2))
    got = lax.all_to_all(sent, ("virt", "y"), 0, 0, tiled=True)
    sent = kernel(sum_kernel, (Z, ROWS + AUX, COLS), (), (got,))
    got = lax.all_to_all(sent, "z", 0, 0, tiled=True)
    scalars = (pair_domain, occ_energy_i, occ_energy_j)
    scale = kernel(scale_kernel, (ROWS, COLS), scalars, (virt_energy[None, :],), dtype=F32)
    return kernel(update_kernel, (1, 1, ROWS, COLS), (), (got, ov, scale))


def solution(mesh):
    fine = Mesh(mesh.devices.reshape(2, VIRT, Y, Z), ("pair", "virt", "y", "z"))
    integ = ("y", "z")
    placed = (
        P("pair", integ, "virt", None),
        P(integ, None, None),
        P(None, integ, None),
        P("pair"),
        P(integ),
        P(),
        P(),
        P("pair", integ, None),
    )
    return jax.shard_map(
        body,
        mesh=fine,
        in_specs=placed,
        out_specs=P("pair", integ, "virt", None),
        check_vma=False,
    )
```

```python
import jax
import jax.numpy as jnp
from jax import lax
from jax.experimental import pallas as pl
from jax.experimental.pallas import tpu as pltpu
from jax.sharding import Mesh
from jax.sharding import PartitionSpec as P

TILE_SIZE = 128
BF16 = jnp.bfloat16
F32 = jnp.float32
NT = (((1,), (1,)), ((), ()))
TN = (((0,), (0,)), ((), ()))
VIRT = 4
Y = 4
Z = 8
ROWS = 64
COLS = 256
AUX = 16
PART = 8
SHARE = 4


def out_kernel(domain_hbm, amp_hbm, ov_hbm, factors_hbm, out_ref, up_ref, down_ref, domain, amp, sems):
    x = lax.axis_index("virt")
    share = lax.axis_index("pair") * SHARE
    copies = [
        pltpu.make_async_copy(domain_hbm.at[0], domain, sems.at[0]),
        pltpu.make_async_copy(amp_hbm.at[0, 0], amp, sems.at[1]),
        pltpu.make_async_copy(factors_hbm.at[pl.ds(share, SHARE)], up_ref, sems.at[2]),
        pltpu.make_async_copy(factors_hbm.at[pl.ds(2 * SHARE + share, SHARE)], down_ref, sems.at[3]),
    ]
    for to in range(Z):
        for high in range(2):
            start = pl.multiple_of(((2 * high + x // 2) * Z + to) * AUX + (x % 2) * PART, PART)
            target = out_ref.at[to, pl.ds(ROWS + high * PART, PART)]
            copies.append(pltpu.make_async_copy(ov_hbm.at[pl.ds(start, PART)], target, sems.at[4 + 2 * to + high]))
    for copy in copies:
        copy.start()
    copies[0].wait()
    copies[1].wait()
    row_tile = domain[0, x // 2]
    for half in range(2):
        cols = slice(half * TILE_SIZE, (half + 1) * TILE_SIZE)
        keep = (row_tile * domain[0, half]).astype(F32)
        rows = (amp[:, cols].astype(F32) * keep).astype(BF16)
        for to in range(Z):
            out_ref[to, :ROWS, cols] = rows
    for copy in copies[2:]:
        copy.wait()


def spread_kernel(got_ref, out_ref):
    for to_x in range(VIRT):
        for to_y in range(Y):
            high, low = divmod(to_y, 2)
            out_ref[to_x * Y + to_y, :ROWS] = got_ref[2 * to_x + low, :ROWS]
            start = ROWS + high * PART
            out_ref[to_x * Y + to_y, ROWS:] = got_ref[2 * to_x + low, start : start + PART]


def ladder_kernel(
    mask_ref, rows_ref, own_ref, up_hbm, down_hbm, up2_hbm, down2_hbm, out_ref, factors, masked, weighted, sems
):
    copies = [
        pltpu.make_async_copy(ref, factors.at[part], sems.at[part])
        for part, ref in enumerate((up_hbm, down_hbm, up2_hbm, down2_hbm))
    ]
    for copy in copies:
        copy.start()

    def mask(slot, matrix):
        for p in range(2):
            for q in range(2):
                keep = jnp.full((1, TILE_SIZE), mask_ref[p, q], jnp.int32).astype(F32).astype(BF16)
                rows = slice(p * TILE_SIZE, (p + 1) * TILE_SIZE)
                left = slot * COLS + q * TILE_SIZE
                block = matrix[rows, q * TILE_SIZE : (q + 1) * TILE_SIZE]
                masked[rows, left : left + TILE_SIZE] = block * keep

    for aux in range(AUX):
        mask(aux, own_ref.at[aux])
    for part, copy in enumerate(copies):
        copy.wait()
        for aux in range(SHARE):
            mask(AUX + part * SHARE + aux, factors.at[part, aux])

    zeta = jnp.zeros((2 * AUX, COLS), F32)
    for at_y in range(Y):
        amp = jnp.concatenate([rows_ref[at_x * Y + at_y, :ROWS] for at_x in range(VIRT)], axis=0)
        fac = jnp.concatenate([rows_ref[at_x * Y + at_y, ROWS:] for at_x in range(VIRT)], axis=0)
        direct = lax.dot_general(fac, amp, NT, preferred_element_type=F32)
        swapped = jnp.dot(fac, amp, preferred_element_type=F32)
        zeta = zeta + (2.0 * direct - swapped)
        for slot in range(2 * AUX):
            cols = slice(slot * COLS, (slot + 1) * COLS)
            weighted[:, cols] = jnp.dot(masked[:, cols], amp, preferred_element_type=F32).astype(BF16)
        total = lax.dot_general(weighted[...], masked[...], NT, preferred_element_type=F32).astype(BF16)
        for at_x in range(VIRT):
            out_ref[at_x * Y + at_y, :ROWS] = total[at_x * ROWS : (at_x + 1) * ROWS]
    group = lax.broadcasted_iota(jnp.int32, (PART, COLS), 1) // ROWS
    for at_x in range(VIRT):
        piece = jnp.zeros((PART, COLS), F32)
        for to in range(4):
            turned = zeta[to * PART : (to + 1) * PART]
            if to != at_x:
                turned = pltpu.roll(turned, ((to - at_x) % 4) * ROWS, 1)
            piece = jnp.where(group == to, turned, piece)
        piece = piece.astype(BF16)
        for at_y in range(Y):
            out_ref[at_x * Y + at_y, ROWS:] = piece


def sum_kernel(got_ref, out_ref):
    sums = [jnp.zeros((PART, COLS), F32), jnp.zeros((PART, COLS), F32)]
    for at_x in range(VIRT):
        for low in range(2):
            first = got_ref[at_x * Y + low]
            second = got_ref[at_x * Y + 2 + low]
            out_ref[2 * at_x + low, :ROWS] = (first[:ROWS].astype(F32) + second[:ROWS].astype(F32)).astype(BF16)
            sums[0] = sums[0] + first[ROWS:].astype(F32)
            sums[1] = sums[1] + second[ROWS:].astype(F32)
    group = lax.broadcasted_iota(jnp.int32, (PART, COLS), 1) // ROWS
    halves = []
    for half in range(2):
        piece = jnp.zeros((PART, COLS), F32)
        for high in range(2):
            for low in range(2):
                source, to = 2 * low + half, 2 * high + low
                turned = sums[high]
                if source != to:
                    turned = pltpu.roll(turned, ((to - source) % 4) * ROWS, 1)
                piece = jnp.where(group == to, turned, piece)
        halves.append(piece)
    zeta = jnp.concatenate(halves, axis=0).astype(BF16)
    for to in range(Z):
        out_ref[to, ROWS:] = zeta


def scale_kernel(domain_ref, occ_i_ref, occ_j_ref, virt_ref, out_ref):
    x = lax.axis_index("virt")
    energy = jnp.broadcast_to(virt_ref[...], (ROWS, COLS))
    row = lax.broadcasted_iota(jnp.int32, (ROWS, COLS), 0) + x * ROWS
    lane = lax.broadcasted_iota(jnp.int32, (ROWS, COLS), 1)
    energy_rows = jnp.sum(jnp.where(row == lane, energy, 0.0), axis=1, keepdims=True)
    denom = energy_rows + energy - occ_i_ref[0] - occ_j_ref[0]
    row_tile = domain_ref[0, 0, x // 2]
    left = (row_tile * domain_ref[0, 0, 0]).astype(F32)
    right = (row_tile * domain_ref[0, 0, 1]).astype(F32)
    out_ref[...] = jnp.where(lane < TILE_SIZE, left, right) / denom


def update_kernel(got_ref, ov_ref, scale_ref, out_ref):
    total = got_ref[0, :ROWS].astype(F32)
    for source in range(1, Z):
        total = total + got_ref[source, :ROWS].astype(F32)
    zeta = got_ref[:, ROWS:].reshape(Z * AUX, COLS)
    for at_y in range(Y):
        part = zeta[:, at_y * ROWS : (at_y + 1) * ROWS]
        fac = ov_ref[at_y * Z * AUX : (at_y + 1) * Z * AUX, :]
        total = total + lax.dot_general(part, fac, TN, preferred_element_type=F32)
    out_ref[0, 0] = (total * scale_ref[...]).astype(BF16)


def kernel(function, shape, scalars, arrays, scratch=(), mib=16, dtype=BF16):
    smem = pl.BlockSpec(memory_space=pltpu.SMEM)
    vmem = pl.BlockSpec(memory_space=pltpu.VMEM)
    call = pl.pallas_call(
        function,
        name=function.__name__,
        in_specs=[smem] * len(scalars) + [vmem] * len(arrays),
        out_specs=vmem,
        out_shape=jax.ShapeDtypeStruct(shape, dtype),
        scratch_shapes=list(scratch),
        compiler_params=pltpu.CompilerParams(vmem_limit_bytes=mib << 20),
    )
    return call(*scalars, *arrays)


def body(
    amplitudes,
    vv_factors,
    ov_factors,
    occ_energy_i,
    occ_energy_j,
    virt_energy,
    vv_mask,
    pair_domain,
):
    ov = ov_factors[:, 0, :]
    hbm = pl.BlockSpec(memory_space=pltpu.HBM)
    vmem = pl.BlockSpec(memory_space=pltpu.VMEM)
    share = jax.ShapeDtypeStruct((SHARE, COLS, COLS), BF16)
    sent, up, down = pl.pallas_call(
        out_kernel,
        name="out_kernel",
        in_specs=[hbm, hbm, hbm, hbm],
        out_specs=[vmem, vmem, vmem],
        out_shape=[jax.ShapeDtypeStruct((Z, ROWS + AUX, COLS), BF16), share, share],
        scratch_shapes=[
            pltpu.SMEM((1, 2), jnp.int32),
            pltpu.VMEM((ROWS, COLS), BF16),
            pltpu.SemaphoreType.DMA((4 + 2 * Z,)),
        ],
    )(pair_domain, amplitudes, ov, vv_factors)
    got = lax.all_to_all(sent, "z", 0, 0, tiled=True)
    sent = kernel(spread_kernel, (VIRT * Y, ROWS + PART, COLS), (), (got,))
    swap = [(0, 1), (1, 0)]
    up = lax.ppermute(up, "y", [(y, (y + 1) % Y) for y in range(Y)])
    down = lax.ppermute(down, "y", [(y, (y - 1) % Y) for y in range(Y)])
    extra = (up, down, lax.ppermute(up, "pair", swap), lax.ppermute(down, "pair", swap))
    got = lax.all_to_all(sent, ("virt", "y"), 0, 0, tiled=True)
    wide = pltpu.VMEM((COLS, 2 * AUX * COLS), BF16)
    sent = pl.pallas_call(
        ladder_kernel,
        name="ladder_kernel",
        in_specs=[pl.BlockSpec(memory_space=pltpu.SMEM)] + [pl.BlockSpec(memory_space=pltpu.VMEM)] * 2 + [hbm] * 4,
        out_specs=pl.BlockSpec(memory_space=pltpu.VMEM),
        out_shape=jax.ShapeDtypeStruct((VIRT * Y, ROWS + PART, COLS), BF16),
        scratch_shapes=[
            pltpu.VMEM((4, SHARE, COLS, COLS), BF16),
            wide,
            wide,
            pltpu.SemaphoreType.DMA((4,)),
        ],
        compiler_params=pltpu.CompilerParams(vmem_limit_bytes=40 << 20),
    )(vv_mask, got, vv_factors, *[pltpu.with_memory_space_constraint(part, pltpu.HBM) for part in extra])
    got = lax.all_to_all(sent, ("virt", "y"), 0, 0, tiled=True)
    sent = kernel(sum_kernel, (Z, ROWS + AUX, COLS), (), (got,))
    got = lax.all_to_all(sent, "z", 0, 0, tiled=True)
    scalars = (pair_domain, occ_energy_i, occ_energy_j)
    scale = kernel(scale_kernel, (ROWS, COLS), scalars, (virt_energy[None, :],), dtype=F32)
    return kernel(update_kernel, (1, 1, ROWS, COLS), (), (got, ov, scale))


def solution(mesh):
    fine = Mesh(mesh.devices.reshape(2, VIRT, Y, Z), ("pair", "virt", "y", "z"))
    integ = ("y", "z")
    placed = (
        P("pair", integ, "virt", None),
        P(integ, None, None),
        P(None, integ, None),
        P("pair"),
        P(integ),
        P(),
        P(),
        P("pair", integ, None),
    )
    return jax.shard_map(
        body,
        mesh=fine,
        in_specs=placed,
        out_specs=P("pair", integ, "virt", None),
        check_vma=False,
    )
```

```python
import jax
import jax.numpy as jnp
from jax import lax
from jax.experimental import pallas as pl
from jax.experimental.pallas import tpu as pltpu
from jax.sharding import Mesh
from jax.sharding import PartitionSpec as P

TILE_SIZE = 128
BF16 = jnp.bfloat16
F32 = jnp.float32
NT = (((1,), (1,)), ((), ()))
TN = (((0,), (0,)), ((), ()))
VIRT = 4
Y = 4
Z = 8
ROWS = 64
COLS = 256
AUX = 16
PART = 8
SHARE = 4


def out_kernel(domain_hbm, amp_hbm, ov_hbm, factors_hbm, out_ref, up_ref, down_ref, domain, amp, sems):
    x = lax.axis_index("virt")
    share = lax.axis_index("pair") * SHARE
    copies = [
        pltpu.make_async_copy(domain_hbm.at[0], domain, sems.at[0]),
        pltpu.make_async_copy(amp_hbm.at[0, 0], amp, sems.at[1]),
        pltpu.make_async_copy(factors_hbm.at[pl.ds(share, SHARE)], up_ref, sems.at[2]),
        pltpu.make_async_copy(factors_hbm.at[pl.ds(2 * SHARE + share, SHARE)], down_ref, sems.at[3]),
    ]
    for to in range(Z):
        for high in range(2):
            start = pl.multiple_of(((2 * high + x // 2) * Z + to) * AUX + (x % 2) * PART, PART)
            target = out_ref.at[to, pl.ds(ROWS + high * PART, PART)]
            copies.append(pltpu.make_async_copy(ov_hbm.at[pl.ds(start, PART)], target, sems.at[4 + 2 * to + high]))
    for copy in copies:
        copy.start()
    copies[0].wait()
    copies[1].wait()
    row_tile = domain[0, x // 2]
    for half in range(2):
        cols = slice(half * TILE_SIZE, (half + 1) * TILE_SIZE)
        keep = (row_tile * domain[0, half]).astype(F32)
        rows = (amp[:, cols].astype(F32) * keep).astype(BF16)
        for to in range(Z):
            out_ref[to, :ROWS, cols] = rows
    for copy in copies[2:]:
        copy.wait()


def spread_kernel(got_ref, out_ref):
    for to_x in range(VIRT):
        for to_y in range(Y):
            high, low = divmod(to_y, 2)
            out_ref[to_x * Y + to_y, :ROWS] = got_ref[2 * to_x + low, :ROWS]
            start = ROWS + high * PART
            out_ref[to_x * Y + to_y, ROWS:] = got_ref[2 * to_x + low, start : start + PART]


def ladder_kernel(
    mask_ref, rows_ref, own_ref, up_hbm, down_hbm, up2_hbm, down2_hbm, out_ref, factors, masked, weighted, sems
):
    copies = [
        pltpu.make_async_copy(ref, factors.at[part], sems.at[part])
        for part, ref in enumerate((up_hbm, down_hbm, up2_hbm, down2_hbm))
    ]
    for copy in copies:
        copy.start()

    def mask(slot, matrix):
        for p in range(2):
            for q in range(2):
                keep = jnp.full((1, TILE_SIZE), mask_ref[p, q], jnp.int32).astype(F32).astype(BF16)
                rows = slice(p * TILE_SIZE, (p + 1) * TILE_SIZE)
                left = slot * COLS + q * TILE_SIZE
                block = matrix[rows, q * TILE_SIZE : (q + 1) * TILE_SIZE]
                masked[rows, left : left + TILE_SIZE] = block * keep

    for aux in range(AUX):
        mask(aux, own_ref.at[aux])
    for part, copy in enumerate(copies):
        copy.wait()
        for aux in range(SHARE):
            mask(AUX + part * SHARE + aux, factors.at[part, aux])

    zeta = jnp.zeros((2 * AUX, COLS), F32)
    for at_y in range(Y):
        amp = jnp.concatenate([rows_ref[at_x * Y + at_y, :ROWS] for at_x in range(VIRT)], axis=0)
        fac = jnp.concatenate([rows_ref[at_x * Y + at_y, ROWS:] for at_x in range(VIRT)], axis=0)
        direct = lax.dot_general(fac, amp, NT, preferred_element_type=F32)
        swapped = jnp.dot(fac, amp, preferred_element_type=F32)
        zeta = zeta + (2.0 * direct - swapped)
        for slot in range(2 * AUX):
            cols = slice(slot * COLS, (slot + 1) * COLS)
            weighted[:, cols] = jnp.dot(masked[:, cols], amp, preferred_element_type=F32).astype(BF16)
        total = lax.dot_general(weighted[...], masked[...], NT, preferred_element_type=F32).astype(BF16)
        for at_x in range(VIRT):
            out_ref[at_x * Y + at_y, :ROWS] = total[at_x * ROWS : (at_x + 1) * ROWS]
    group = lax.broadcasted_iota(jnp.int32, (PART, COLS), 1) // ROWS
    for at_x in range(VIRT):
        piece = jnp.zeros((PART, COLS), F32)
        for to in range(4):
            turned = zeta[to * PART : (to + 1) * PART]
            if to != at_x:
                turned = pltpu.roll(turned, ((to - at_x) % 4) * ROWS, 1)
            piece = jnp.where(group == to, turned, piece)
        piece = piece.astype(BF16)
        for at_y in range(Y):
            out_ref[at_x * Y + at_y, ROWS:] = piece


def sum_kernel(got_ref, out_ref):
    sums = [jnp.zeros((PART, COLS), F32), jnp.zeros((PART, COLS), F32)]
    for at_x in range(VIRT):
        for low in range(2):
            first = got_ref[at_x * Y + low]
            second = got_ref[at_x * Y + 2 + low]
            out_ref[2 * at_x + low, :ROWS] = (first[:ROWS].astype(F32) + second[:ROWS].astype(F32)).astype(BF16)
            sums[0] = sums[0] + first[ROWS:].astype(F32)
            sums[1] = sums[1] + second[ROWS:].astype(F32)
    group = lax.broadcasted_iota(jnp.int32, (PART, COLS), 1) // ROWS
    halves = []
    for half in range(2):
        piece = jnp.zeros((PART, COLS), F32)
        for high in range(2):
            for low in range(2):
                source, to = 2 * low + half, 2 * high + low
                turned = sums[high]
                if source != to:
                    turned = pltpu.roll(turned, ((to - source) % 4) * ROWS, 1)
                piece = jnp.where(group == to, turned, piece)
        halves.append(piece)
    zeta = jnp.concatenate(halves, axis=0).astype(BF16)
    for to in range(Z):
        out_ref[to, ROWS:] = zeta


def scale_kernel(domain_ref, occ_i_ref, occ_j_ref, virt_ref, out_ref):
    x = lax.axis_index("virt")
    energy = jnp.broadcast_to(virt_ref[...], (ROWS, COLS))
    row = lax.broadcasted_iota(jnp.int32, (ROWS, COLS), 0) + x * ROWS
    lane = lax.broadcasted_iota(jnp.int32, (ROWS, COLS), 1)
    energy_rows = jnp.sum(jnp.where(row == lane, energy, 0.0), axis=1, keepdims=True)
    denom = energy_rows + energy - occ_i_ref[0] - occ_j_ref[0]
    row_tile = domain_ref[0, 0, x // 2]
    left = (row_tile * domain_ref[0, 0, 0]).astype(F32)
    right = (row_tile * domain_ref[0, 0, 1]).astype(F32)
    out_ref[...] = jnp.where(lane < TILE_SIZE, left, right) / denom


def update_kernel(got_ref, ov_ref, scale_ref, out_ref):
    total = got_ref[0, :ROWS].astype(F32)
    for source in range(1, Z):
        total = total + got_ref[source, :ROWS].astype(F32)
    zeta = got_ref[:, ROWS:].reshape(Z * AUX, COLS)
    for at_y in range(Y):
        part = zeta[:, at_y * ROWS : (at_y + 1) * ROWS]
        fac = ov_ref[at_y * Z * AUX : (at_y + 1) * Z * AUX, :]
        total = total + lax.dot_general(part, fac, TN, preferred_element_type=F32)
    out_ref[0, 0] = (total * scale_ref[...]).astype(BF16)


def kernel(function, shape, scalars, arrays, scratch=(), mib=16, dtype=BF16):
    smem = pl.BlockSpec(memory_space=pltpu.SMEM)
    vmem = pl.BlockSpec(memory_space=pltpu.VMEM)
    call = pl.pallas_call(
        function,
        name=function.__name__,
        in_specs=[smem] * len(scalars) + [vmem] * len(arrays),
        out_specs=vmem,
        out_shape=jax.ShapeDtypeStruct(shape, dtype),
        scratch_shapes=list(scratch),
        compiler_params=pltpu.CompilerParams(vmem_limit_bytes=mib << 20),
    )
    return call(*scalars, *arrays)


def body(
    amplitudes,
    vv_factors,
    ov_factors,
    occ_energy_i,
    occ_energy_j,
    virt_energy,
    vv_mask,
    pair_domain,
):
    ov = ov_factors[:, 0, :]
    hbm = pl.BlockSpec(memory_space=pltpu.HBM)
    vmem = pl.BlockSpec(memory_space=pltpu.VMEM)
    share = jax.ShapeDtypeStruct((SHARE, COLS, COLS), BF16)
    sent, up, down = pl.pallas_call(
        out_kernel,
        name="out_kernel",
        in_specs=[hbm, hbm, hbm, hbm],
        out_specs=[vmem, vmem, vmem],
        out_shape=[jax.ShapeDtypeStruct((Z, ROWS + AUX, COLS), BF16), share, share],
        scratch_shapes=[
            pltpu.SMEM((1, 2), jnp.int32),
            pltpu.VMEM((ROWS, COLS), BF16),
            pltpu.SemaphoreType.DMA((4 + 2 * Z,)),
        ],
    )(pair_domain, amplitudes, ov, vv_factors)
    got = lax.all_to_all(sent, "z", 0, 0, tiled=True)
    sent = kernel(spread_kernel, (VIRT * Y, ROWS + PART, COLS), (), (got,))
    swap = [(0, 1), (1, 0)]
    up = lax.ppermute(up, "y", [(y, (y + 1) % Y) for y in range(Y)])
    down = lax.ppermute(down, "y", [(y, (y - 1) % Y) for y in range(Y)])
    extra = (up, down, lax.ppermute(up, "pair", swap), lax.ppermute(down, "pair", swap))
    got = lax.all_to_all(sent, ("virt", "y"), 0, 0, tiled=True)
    wide = pltpu.VMEM((COLS, 2 * AUX * COLS), BF16)
    sent = pl.pallas_call(
        ladder_kernel,
        name="ladder_kernel",
        in_specs=[pl.BlockSpec(memory_space=pltpu.SMEM)] + [pl.BlockSpec(memory_space=pltpu.VMEM)] * 2 + [hbm] * 4,
        out_specs=pl.BlockSpec(memory_space=pltpu.VMEM),
        out_shape=jax.ShapeDtypeStruct((VIRT * Y, ROWS + PART, COLS), BF16),
        scratch_shapes=[
            pltpu.VMEM((4, SHARE, COLS, COLS), BF16),
            wide,
            wide,
            pltpu.SemaphoreType.DMA((4,)),
        ],
        compiler_params=pltpu.CompilerParams(vmem_limit_bytes=40 << 20),
    )(vv_mask, got, vv_factors, *[pltpu.with_memory_space_constraint(part, pltpu.HBM) for part in extra])
    scalars = (pair_domain, occ_energy_i, occ_energy_j)
    scale = kernel(scale_kernel, (ROWS, COLS), scalars, (virt_energy[None, :],), dtype=F32)
    sent, scale = lax.optimization_barrier((sent, scale))
    got = lax.all_to_all(sent, ("virt", "y"), 0, 0, tiled=True)
    sent = kernel(sum_kernel, (Z, ROWS + AUX, COLS), (), (got,))
    got = lax.all_to_all(sent, "z", 0, 0, tiled=True)
    return kernel(update_kernel, (1, 1, ROWS, COLS), (), (got, ov, scale))


def solution(mesh):
    fine = Mesh(mesh.devices.reshape(2, VIRT, Y, Z), ("pair", "virt", "y", "z"))
    integ = ("y", "z")
    placed = (
        P("pair", integ, "virt", None),
        P(integ, None, None),
        P(None, integ, None),
        P("pair"),
        P(integ),
        P(),
        P(),
        P("pair", integ, None),
    )
    return jax.shard_map(
        body,
        mesh=fine,
        in_specs=placed,
        out_specs=P("pair", integ, "virt", None),
        check_vma=False,
    )
```

```python
import jax
import jax.numpy as jnp
from jax import lax
from jax.experimental import pallas as pl
from jax.experimental.pallas import tpu as pltpu
from jax.sharding import Mesh
from jax.sharding import PartitionSpec as P

TILE_SIZE = 128
BF16 = jnp.bfloat16
F32 = jnp.float32
NT = (((1,), (1,)), ((), ()))
TN = (((0,), (0,)), ((), ()))
VIRT = 4
Y = 4
Z = 8
ROWS = 64
COLS = 256
AUX = 16
PART = 8
SHARE = 4


def out_kernel(domain_hbm, amp_hbm, ov_hbm, out_ref, domain, amp, sems):
    x = lax.axis_index("virt")
    copies = [
        pltpu.make_async_copy(domain_hbm.at[0], domain, sems.at[0]),
        pltpu.make_async_copy(amp_hbm.at[0, 0], amp, sems.at[1]),
    ]
    for to in range(Z):
        for high in range(2):
            start = pl.multiple_of(((2 * high + x // 2) * Z + to) * AUX + (x % 2) * PART, PART)
            target = out_ref.at[to, pl.ds(ROWS + high * PART, PART)]
            copies.append(pltpu.make_async_copy(ov_hbm.at[pl.ds(start, PART)], target, sems.at[2 + 2 * to + high]))
    for copy in copies:
        copy.start()
    copies[0].wait()
    copies[1].wait()
    row_tile = domain[0, x // 2]
    for half in range(2):
        cols = slice(half * TILE_SIZE, (half + 1) * TILE_SIZE)
        keep = (row_tile * domain[0, half]).astype(F32)
        rows = (amp[:, cols].astype(F32) * keep).astype(BF16)
        for to in range(Z):
            out_ref[to, :ROWS, cols] = rows
    for copy in copies[2:]:
        copy.wait()


def share_kernel(factors_hbm, up_ref, down_ref, sems):
    share = lax.axis_index("pair") * SHARE
    up = pltpu.make_async_copy(factors_hbm.at[pl.ds(share, SHARE)], up_ref, sems.at[0])
    down = pltpu.make_async_copy(factors_hbm.at[pl.ds(2 * SHARE + share, SHARE)], down_ref, sems.at[1])
    up.start()
    down.start()
    up.wait()
    down.wait()


def spread_kernel(got_ref, out_ref):
    for to_x in range(VIRT):
        for to_y in range(Y):
            high, low = divmod(to_y, 2)
            out_ref[to_x * Y + to_y, :ROWS] = got_ref[2 * to_x + low, :ROWS]
            start = ROWS + high * PART
            out_ref[to_x * Y + to_y, ROWS:] = got_ref[2 * to_x + low, start : start + PART]


def ladder_kernel(
    mask_ref, rows_ref, own_ref, up_hbm, down_hbm, up2_hbm, down2_hbm, out_ref, factors, masked, weighted, sems
):
    copies = [
        pltpu.make_async_copy(ref, factors.at[part], sems.at[part])
        for part, ref in enumerate((up_hbm, down_hbm, up2_hbm, down2_hbm))
    ]
    for copy in copies:
        copy.start()

    def mask(slot, matrix):
        for p in range(2):
            for q in range(2):
                keep = jnp.full((1, TILE_SIZE), mask_ref[p, q], jnp.int32).astype(F32).astype(BF16)
                rows = slice(p * TILE_SIZE, (p + 1) * TILE_SIZE)
                left = slot * COLS + q * TILE_SIZE
                block = matrix[rows, q * TILE_SIZE : (q + 1) * TILE_SIZE]
                masked[rows, left : left + TILE_SIZE] = block * keep

    zeta = jnp.zeros((2 * AUX, COLS), F32)
    for at_y in range(Y):
        amp = jnp.concatenate([rows_ref[at_x * Y + at_y, :ROWS] for at_x in range(VIRT)], axis=0)
        fac = jnp.concatenate([rows_ref[at_x * Y + at_y, ROWS:] for at_x in range(VIRT)], axis=0)
        direct = lax.dot_general(fac, amp, NT, preferred_element_type=F32)
        swapped = jnp.dot(fac, amp, preferred_element_type=F32)
        zeta = zeta + (2.0 * direct - swapped)
        for aux in range(at_y * SHARE, (at_y + 1) * SHARE):
            mask(aux, own_ref.at[aux])
    for copy in copies:
        copy.wait()
    for at_y in range(Y):
        amp = jnp.concatenate([rows_ref[at_x * Y + at_y, :ROWS] for at_x in range(VIRT)], axis=0)
        for slot in range(2 * AUX):
            cols = slice(slot * COLS, (slot + 1) * COLS)
            weighted[:, cols] = jnp.dot(masked[:, cols], amp, preferred_element_type=F32).astype(BF16)
            if at_y == 0 and slot < AUX:
                mask(AUX + slot, factors.at[slot // SHARE, slot % SHARE])
        total = lax.dot_general(weighted[...], masked[...], NT, preferred_element_type=F32).astype(BF16)
        for at_x in range(VIRT):
            out_ref[at_x * Y + at_y, :ROWS] = total[at_x * ROWS : (at_x + 1) * ROWS]
    group = lax.broadcasted_iota(jnp.int32, (PART, COLS), 1) // ROWS
    for at_x in range(VIRT):
        piece = jnp.zeros((PART, COLS), F32)
        for to in range(4):
            turned = zeta[to * PART : (to + 1) * PART]
            if to != at_x:
                turned = pltpu.roll(turned, ((to - at_x) % 4) * ROWS, 1)
            piece = jnp.where(group == to, turned, piece)
        piece = piece.astype(BF16)
        for at_y in range(Y):
            out_ref[at_x * Y + at_y, ROWS:] = piece


def sum_kernel(got_ref, out_ref):
    sums = [jnp.zeros((PART, COLS), F32), jnp.zeros((PART, COLS), F32)]
    for at_x in range(VIRT):
        for low in range(2):
            first = got_ref[at_x * Y + low]
            second = got_ref[at_x * Y + 2 + low]
            out_ref[2 * at_x + low, :ROWS] = (first[:ROWS].astype(F32) + second[:ROWS].astype(F32)).astype(BF16)
            sums[0] = sums[0] + first[ROWS:].astype(F32)
            sums[1] = sums[1] + second[ROWS:].astype(F32)
    group = lax.broadcasted_iota(jnp.int32, (PART, COLS), 1) // ROWS
    halves = []
    for half in range(2):
        piece = jnp.zeros((PART, COLS), F32)
        for high in range(2):
            for low in range(2):
                source, to = 2 * low + half, 2 * high + low
                turned = sums[high]
                if source != to:
                    turned = pltpu.roll(turned, ((to - source) % 4) * ROWS, 1)
                piece = jnp.where(group == to, turned, piece)
        halves.append(piece)
    zeta = jnp.concatenate(halves, axis=0).astype(BF16)
    for to in range(Z):
        out_ref[to, ROWS:] = zeta


def scale_kernel(domain_ref, occ_i_ref, occ_j_ref, virt_ref, out_ref):
    x = lax.axis_index("virt")
    energy = jnp.broadcast_to(virt_ref[...], (ROWS, COLS))
    row = lax.broadcasted_iota(jnp.int32, (ROWS, COLS), 0) + x * ROWS
    lane = lax.broadcasted_iota(jnp.int32, (ROWS, COLS), 1)
    energy_rows = jnp.sum(jnp.where(row == lane, energy, 0.0), axis=1, keepdims=True)
    denom = energy_rows + energy - occ_i_ref[0] - occ_j_ref[0]
    row_tile = domain_ref[0, 0, x // 2]
    left = (row_tile * domain_ref[0, 0, 0]).astype(F32)
    right = (row_tile * domain_ref[0, 0, 1]).astype(F32)
    out_ref[...] = jnp.where(lane < TILE_SIZE, left, right) / denom


def update_kernel(got_ref, ov_ref, scale_ref, out_ref):
    total = got_ref[0, :ROWS].astype(F32)
    for source in range(1, Z):
        total = total + got_ref[source, :ROWS].astype(F32)
    zeta = got_ref[:, ROWS:].reshape(Z * AUX, COLS)
    for at_y in range(Y):
        part = zeta[:, at_y * ROWS : (at_y + 1) * ROWS]
        fac = ov_ref[at_y * Z * AUX : (at_y + 1) * Z * AUX, :]
        total = total + lax.dot_general(part, fac, TN, preferred_element_type=F32)
    out_ref[0, 0] = (total * scale_ref[...]).astype(BF16)


def kernel(function, shape, scalars, arrays, scratch=(), mib=16, dtype=BF16):
    smem = pl.BlockSpec(memory_space=pltpu.SMEM)
    vmem = pl.BlockSpec(memory_space=pltpu.VMEM)
    call = pl.pallas_call(
        function,
        name=function.__name__,
        in_specs=[smem] * len(scalars) + [vmem] * len(arrays),
        out_specs=vmem,
        out_shape=jax.ShapeDtypeStruct(shape, dtype),
        scratch_shapes=list(scratch),
        compiler_params=pltpu.CompilerParams(vmem_limit_bytes=mib << 20),
    )
    return call(*scalars, *arrays)


def body(
    amplitudes,
    vv_factors,
    ov_factors,
    occ_energy_i,
    occ_energy_j,
    virt_energy,
    vv_mask,
    pair_domain,
):
    ov = ov_factors[:, 0, :]
    hbm = pl.BlockSpec(memory_space=pltpu.HBM)
    sent = pl.pallas_call(
        out_kernel,
        name="out_kernel",
        in_specs=[hbm, hbm, hbm],
        out_specs=pl.BlockSpec(memory_space=pltpu.VMEM),
        out_shape=jax.ShapeDtypeStruct((Z, ROWS + AUX, COLS), BF16),
        scratch_shapes=[
            pltpu.SMEM((1, 2), jnp.int32),
            pltpu.VMEM((ROWS, COLS), BF16),
            pltpu.SemaphoreType.DMA((2 + 2 * Z,)),
        ],
    )(pair_domain, amplitudes, ov)
    up, down = pl.pallas_call(
        share_kernel,
        name="share_kernel",
        in_specs=[hbm],
        out_specs=[pl.BlockSpec(memory_space=pltpu.VMEM)] * 2,
        out_shape=[jax.ShapeDtypeStruct((SHARE, COLS, COLS), BF16)] * 2,
        scratch_shapes=[pltpu.SemaphoreType.DMA((2,))],
    )(vv_factors)
    got = lax.all_to_all(sent, "z", 0, 0, tiled=True)
    sent = kernel(spread_kernel, (VIRT * Y, ROWS + PART, COLS), (), (got,))
    swap = [(0, 1), (1, 0)]
    up = lax.ppermute(up, "y", [(y, (y + 1) % Y) for y in range(Y)])
    down = lax.ppermute(down, "y", [(y, (y - 1) % Y) for y in range(Y)])
    extra = (up, down, lax.ppermute(up, "pair", swap), lax.ppermute(down, "pair", swap))
    got = lax.all_to_all(sent, ("virt", "y"), 0, 0, tiled=True)
    wide = pltpu.VMEM((COLS, 2 * AUX * COLS), BF16)
    sent = pl.pallas_call(
        ladder_kernel,
        name="ladder_kernel",
        in_specs=[pl.BlockSpec(memory_space=pltpu.SMEM)] + [pl.BlockSpec(memory_space=pltpu.VMEM)] * 2 + [hbm] * 4,
        out_specs=pl.BlockSpec(memory_space=pltpu.VMEM),
        out_shape=jax.ShapeDtypeStruct((VIRT * Y, ROWS + PART, COLS), BF16),
        scratch_shapes=[
            pltpu.VMEM((4, SHARE, COLS, COLS), BF16),
            wide,
            wide,
            pltpu.SemaphoreType.DMA((4,)),
        ],
        compiler_params=pltpu.CompilerParams(vmem_limit_bytes=40 << 20),
    )(vv_mask, got, vv_factors, *[pltpu.with_memory_space_constraint(part, pltpu.HBM) for part in extra])
    scalars = (pair_domain, occ_energy_i, occ_energy_j)
    scale = kernel(scale_kernel, (ROWS, COLS), scalars, (virt_energy[None, :],), dtype=F32)
    sent, scale = lax.optimization_barrier((sent, scale))
    got = lax.all_to_all(sent, ("virt", "y"), 0, 0, tiled=True)
    sent = kernel(sum_kernel, (Z, ROWS + AUX, COLS), (), (got,))
    got = lax.all_to_all(sent, "z", 0, 0, tiled=True)
    return kernel(update_kernel, (1, 1, ROWS, COLS), (), (got, ov, scale))


def solution(mesh):
    fine = Mesh(mesh.devices.reshape(2, VIRT, Y, Z), ("pair", "virt", "y", "z"))
    integ = ("y", "z")
    placed = (
        P("pair", integ, "virt", None),
        P(integ, None, None),
        P(None, integ, None),
        P("pair"),
        P(integ),
        P(),
        P(),
        P("pair", integ, None),
    )
    return jax.shard_map(
        body,
        mesh=fine,
        in_specs=placed,
        out_specs=P("pair", integ, "virt", None),
        check_vma=False,
    )
```

```python
import jax
import jax.numpy as jnp
from jax import lax
from jax.experimental import pallas as pl
from jax.experimental.pallas import tpu as pltpu
from jax.sharding import Mesh
from jax.sharding import PartitionSpec as P

TILE_SIZE = 128
BF16 = jnp.bfloat16
F32 = jnp.float32
NT = (((1,), (1,)), ((), ()))
TN = (((0,), (0,)), ((), ()))
VIRT = 4
Y = 4
Z = 8
ROWS = 64
COLS = 256
AUX = 16
PART = 8
SHARE = 4


def out_kernel(domain_hbm, amp_hbm, ov_hbm, factors_hbm, out_ref, up_hbm, down_hbm, domain, amp, shares, sems):
    x = lax.axis_index("virt")
    share = lax.axis_index("pair") * SHARE
    copies = [
        pltpu.make_async_copy(domain_hbm.at[0], domain, sems.at[0]),
        pltpu.make_async_copy(amp_hbm.at[0, 0], amp, sems.at[1]),
        pltpu.make_async_copy(factors_hbm.at[pl.ds(share, SHARE)], shares.at[0], sems.at[2]),
        pltpu.make_async_copy(factors_hbm.at[pl.ds(2 * SHARE + share, SHARE)], shares.at[1], sems.at[3]),
    ]
    for to in range(Z):
        for high in range(2):
            start = pl.multiple_of(((2 * high + x // 2) * Z + to) * AUX + (x % 2) * PART, PART)
            target = out_ref.at[to, pl.ds(ROWS + high * PART, PART)]
            copies.append(pltpu.make_async_copy(ov_hbm.at[pl.ds(start, PART)], target, sems.at[4 + 2 * to + high]))
    for copy in copies:
        copy.start()
    copies[0].wait()
    copies[1].wait()
    row_tile = domain[0, x // 2]
    for half in range(2):
        cols = slice(half * TILE_SIZE, (half + 1) * TILE_SIZE)
        keep = (row_tile * domain[0, half]).astype(F32)
        rows = (amp[:, cols].astype(F32) * keep).astype(BF16)
        for to in range(Z):
            out_ref[to, :ROWS, cols] = rows
    writes = []
    for part, target in enumerate((up_hbm, down_hbm)):
        copies[2 + part].wait()
        writes.append(pltpu.make_async_copy(shares.at[part], target, sems.at[4 + 2 * Z + part]))
        writes[-1].start()
    for copy in copies[4:] + writes:
        copy.wait()


def spread_kernel(got_ref, out_ref):
    for to_x in range(VIRT):
        for to_y in range(Y):
            high, low = divmod(to_y, 2)
            out_ref[to_x * Y + to_y, :ROWS] = got_ref[2 * to_x + low, :ROWS]
            start = ROWS + high * PART
            out_ref[to_x * Y + to_y, ROWS:] = got_ref[2 * to_x + low, start : start + PART]


def ladder_kernel(
    mask_ref, rows_ref, own_ref, up_hbm, down_hbm, up2_hbm, down2_hbm, out_ref, factors, masked, weighted, sems
):
    copies = [
        pltpu.make_async_copy(ref, factors.at[part], sems.at[part])
        for part, ref in enumerate((up_hbm, down_hbm, up2_hbm, down2_hbm))
    ]
    for copy in copies:
        copy.start()

    def mask(slot, matrix):
        for p in range(2):
            for q in range(2):
                keep = jnp.full((1, TILE_SIZE), mask_ref[p, q], jnp.int32).astype(F32).astype(BF16)
                rows = slice(p * TILE_SIZE, (p + 1) * TILE_SIZE)
                left = slot * COLS + q * TILE_SIZE
                block = matrix[rows, q * TILE_SIZE : (q + 1) * TILE_SIZE]
                masked[rows, left : left + TILE_SIZE] = block * keep

    for aux in range(AUX):
        mask(aux, own_ref.at[aux])
    for part, copy in enumerate(copies):
        copy.wait()
        for aux in range(SHARE):
            mask(AUX + part * SHARE + aux, factors.at[part, aux])

    zeta = jnp.zeros((2 * AUX, COLS), F32)
    for at_y in range(Y):
        amp = jnp.concatenate([rows_ref[at_x * Y + at_y, :ROWS] for at_x in range(VIRT)], axis=0)
        fac = jnp.concatenate([rows_ref[at_x * Y + at_y, ROWS:] for at_x in range(VIRT)], axis=0)
        direct = lax.dot_general(fac, amp, NT, preferred_element_type=F32)
        swapped = jnp.dot(fac, amp, preferred_element_type=F32)
        zeta = zeta + (2.0 * direct - swapped)
        for slot in range(2 * AUX):
            cols = slice(slot * COLS, (slot + 1) * COLS)
            weighted[:, cols] = jnp.dot(masked[:, cols], amp, preferred_element_type=F32).astype(BF16)
        total = lax.dot_general(weighted[...], masked[...], NT, preferred_element_type=F32).astype(BF16)
        for at_x in range(VIRT):
            out_ref[at_x * Y + at_y, :ROWS] = total[at_x * ROWS : (at_x + 1) * ROWS]
    group = lax.broadcasted_iota(jnp.int32, (PART, COLS), 1) // ROWS
    for at_x in range(VIRT):
        piece = jnp.zeros((PART, COLS), F32)
        for to in range(4):
            turned = zeta[to * PART : (to + 1) * PART]
            if to != at_x:
                turned = pltpu.roll(turned, ((to - at_x) % 4) * ROWS, 1)
            piece = jnp.where(group == to, turned, piece)
        piece = piece.astype(BF16)
        for at_y in range(Y):
            out_ref[at_x * Y + at_y, ROWS:] = piece


def sum_kernel(got_ref, out_ref):
    sums = [jnp.zeros((PART, COLS), F32), jnp.zeros((PART, COLS), F32)]
    for at_x in range(VIRT):
        for low in range(2):
            first = got_ref[at_x * Y + low]
            second = got_ref[at_x * Y + 2 + low]
            out_ref[2 * at_x + low, :ROWS] = (first[:ROWS].astype(F32) + second[:ROWS].astype(F32)).astype(BF16)
            sums[0] = sums[0] + first[ROWS:].astype(F32)
            sums[1] = sums[1] + second[ROWS:].astype(F32)
    group = lax.broadcasted_iota(jnp.int32, (PART, COLS), 1) // ROWS
    halves = []
    for half in range(2):
        piece = jnp.zeros((PART, COLS), F32)
        for high in range(2):
            for low in range(2):
                source, to = 2 * low + half, 2 * high + low
                turned = sums[high]
                if source != to:
                    turned = pltpu.roll(turned, ((to - source) % 4) * ROWS, 1)
                piece = jnp.where(group == to, turned, piece)
        halves.append(piece)
    zeta = jnp.concatenate(halves, axis=0).astype(BF16)
    for to in range(Z):
        out_ref[to, ROWS:] = zeta


def scale_kernel(domain_ref, occ_i_ref, occ_j_ref, virt_ref, out_ref):
    x = lax.axis_index("virt")
    energy = jnp.broadcast_to(virt_ref[...], (ROWS, COLS))
    row = lax.broadcasted_iota(jnp.int32, (ROWS, COLS), 0) + x * ROWS
    lane = lax.broadcasted_iota(jnp.int32, (ROWS, COLS), 1)
    energy_rows = jnp.sum(jnp.where(row == lane, energy, 0.0), axis=1, keepdims=True)
    denom = energy_rows + energy - occ_i_ref[0] - occ_j_ref[0]
    row_tile = domain_ref[0, 0, x // 2]
    left = (row_tile * domain_ref[0, 0, 0]).astype(F32)
    right = (row_tile * domain_ref[0, 0, 1]).astype(F32)
    out_ref[...] = jnp.where(lane < TILE_SIZE, left, right) / denom


def update_kernel(got_ref, ov_ref, scale_ref, out_ref):
    total = got_ref[0, :ROWS].astype(F32)
    for source in range(1, Z):
        total = total + got_ref[source, :ROWS].astype(F32)
    zeta = got_ref[:, ROWS:].reshape(Z * AUX, COLS)
    for at_y in range(Y):
        part = zeta[:, at_y * ROWS : (at_y + 1) * ROWS]
        fac = ov_ref[at_y * Z * AUX : (at_y + 1) * Z * AUX, :]
        total = total + lax.dot_general(part, fac, TN, preferred_element_type=F32)
    out_ref[0, 0] = (total * scale_ref[...]).astype(BF16)


def kernel(function, shape, scalars, arrays, scratch=(), mib=16, dtype=BF16):
    smem = pl.BlockSpec(memory_space=pltpu.SMEM)
    vmem = pl.BlockSpec(memory_space=pltpu.VMEM)
    call = pl.pallas_call(
        function,
        name=function.__name__,
        in_specs=[smem] * len(scalars) + [vmem] * len(arrays),
        out_specs=vmem,
        out_shape=jax.ShapeDtypeStruct(shape, dtype),
        scratch_shapes=list(scratch),
        compiler_params=pltpu.CompilerParams(vmem_limit_bytes=mib << 20),
    )
    return call(*scalars, *arrays)


def body(
    amplitudes,
    vv_factors,
    ov_factors,
    occ_energy_i,
    occ_energy_j,
    virt_energy,
    vv_mask,
    pair_domain,
):
    ov = ov_factors[:, 0, :]
    hbm = pl.BlockSpec(memory_space=pltpu.HBM)
    vmem = pl.BlockSpec(memory_space=pltpu.VMEM)
    share = jax.ShapeDtypeStruct((SHARE, COLS, COLS), BF16)
    sent, up, down = pl.pallas_call(
        out_kernel,
        name="out_kernel",
        in_specs=[hbm, hbm, hbm, hbm],
        out_specs=[vmem, hbm, hbm],
        out_shape=[jax.ShapeDtypeStruct((Z, ROWS + AUX, COLS), BF16), share, share],
        scratch_shapes=[
            pltpu.SMEM((1, 2), jnp.int32),
            pltpu.VMEM((ROWS, COLS), BF16),
            pltpu.VMEM((2, SHARE, COLS, COLS), BF16),
            pltpu.SemaphoreType.DMA((6 + 2 * Z,)),
        ],
    )(pair_domain, amplitudes, ov, vv_factors)
    got = lax.all_to_all(sent, "z", 0, 0, tiled=True)
    sent = kernel(spread_kernel, (VIRT * Y, ROWS + PART, COLS), (), (got,))
    swap = [(0, 1), (1, 0)]
    up = lax.ppermute(up, "y", [(y, (y + 1) % Y) for y in range(Y)])
    down = lax.ppermute(down, "y", [(y, (y - 1) % Y) for y in range(Y)])
    extra = (up, down, lax.ppermute(up, "pair", swap), lax.ppermute(down, "pair", swap))
    got = lax.all_to_all(sent, ("virt", "y"), 0, 0, tiled=True)
    wide = pltpu.VMEM((COLS, 2 * AUX * COLS), BF16)
    sent = pl.pallas_call(
        ladder_kernel,
        name="ladder_kernel",
        in_specs=[pl.BlockSpec(memory_space=pltpu.SMEM)] + [pl.BlockSpec(memory_space=pltpu.VMEM)] * 2 + [hbm] * 4,
        out_specs=pl.BlockSpec(memory_space=pltpu.VMEM),
        out_shape=jax.ShapeDtypeStruct((VIRT * Y, ROWS + PART, COLS), BF16),
        scratch_shapes=[
            pltpu.VMEM((4, SHARE, COLS, COLS), BF16),
            wide,
            wide,
            pltpu.SemaphoreType.DMA((4,)),
        ],
        compiler_params=pltpu.CompilerParams(vmem_limit_bytes=40 << 20),
    )(vv_mask, got, vv_factors, *[pltpu.with_memory_space_constraint(part, pltpu.HBM) for part in extra])
    scalars = (pair_domain, occ_energy_i, occ_energy_j)
    scale = kernel(scale_kernel, (ROWS, COLS), scalars, (virt_energy[None, :],), dtype=F32)
    sent, scale = lax.optimization_barrier((sent, scale))
    got = lax.all_to_all(sent, ("virt", "y"), 0, 0, tiled=True)
    sent = kernel(sum_kernel, (Z, ROWS + AUX, COLS), (), (got,))
    got = lax.all_to_all(sent, "z", 0, 0, tiled=True)
    return kernel(update_kernel, (1, 1, ROWS, COLS), (), (got, ov, scale))


def solution(mesh):
    fine = Mesh(mesh.devices.reshape(2, VIRT, Y, Z), ("pair", "virt", "y", "z"))
    integ = ("y", "z")
    placed = (
        P("pair", integ, "virt", None),
        P(integ, None, None),
        P(None, integ, None),
        P("pair"),
        P(integ),
        P(),
        P(),
        P("pair", integ, None),
    )
    return jax.shard_map(
        body,
        mesh=fine,
        in_specs=placed,
        out_specs=P("pair", integ, "virt", None),
        check_vma=False,
    )
```

```python
import jax
import jax.numpy as jnp
from jax import lax
from jax.experimental import pallas as pl
from jax.experimental.pallas import tpu as pltpu
from jax.sharding import Mesh
from jax.sharding import PartitionSpec as P

TILE_SIZE = 128
BF16 = jnp.bfloat16
F32 = jnp.float32
NT = (((1,), (1,)), ((), ()))
TN = (((0,), (0,)), ((), ()))
VIRT = 4
Y = 4
Z = 8
ROWS = 64
COLS = 256
AUX = 16
PART = 8
SHARE = 4


def out_kernel(domain_hbm, amp_hbm, ov_hbm, factors_hbm, out_ref, up_ref, domain, amp, sems):
    x = lax.axis_index("virt")
    share = lax.axis_index("pair") * SHARE
    copies = [
        pltpu.make_async_copy(domain_hbm.at[0], domain, sems.at[0]),
        pltpu.make_async_copy(amp_hbm.at[0, 0], amp, sems.at[1]),
        pltpu.make_async_copy(factors_hbm.at[pl.ds(share, SHARE)], up_ref, sems.at[2]),
    ]
    for to in range(Z):
        for high in range(2):
            start = pl.multiple_of(((2 * high + x // 2) * Z + to) * AUX + (x % 2) * PART, PART)
            target = out_ref.at[to, pl.ds(ROWS + high * PART, PART)]
            copies.append(pltpu.make_async_copy(ov_hbm.at[pl.ds(start, PART)], target, sems.at[3 + 2 * to + high]))
    for copy in copies:
        copy.start()
    copies[0].wait()
    copies[1].wait()
    row_tile = domain[0, x // 2]
    for half in range(2):
        cols = slice(half * TILE_SIZE, (half + 1) * TILE_SIZE)
        keep = (row_tile * domain[0, half]).astype(F32)
        rows = (amp[:, cols].astype(F32) * keep).astype(BF16)
        for to in range(Z):
            out_ref[to, :ROWS, cols] = rows
    for copy in copies[2:]:
        copy.wait()


def down_kernel(factors_hbm, down_ref, sem):
    share = lax.axis_index("pair") * SHARE
    copy = pltpu.make_async_copy(factors_hbm.at[pl.ds(2 * SHARE + share, SHARE)], down_ref, sem)
    copy.start()
    copy.wait()


def spread_kernel(got_ref, out_ref):
    for to_x in range(VIRT):
        for to_y in range(Y):
            high, low = divmod(to_y, 2)
            out_ref[to_x * Y + to_y, :ROWS] = got_ref[2 * to_x + low, :ROWS]
            start = ROWS + high * PART
            out_ref[to_x * Y + to_y, ROWS:] = got_ref[2 * to_x + low, start : start + PART]


def ladder_kernel(
    mask_ref, rows_ref, own_ref, up_hbm, down_hbm, up2_hbm, down2_hbm, out_ref, factors, masked, weighted, sems
):
    copies = [
        pltpu.make_async_copy(ref, factors.at[part], sems.at[part])
        for part, ref in enumerate((up_hbm, down_hbm, up2_hbm, down2_hbm))
    ]
    for copy in copies:
        copy.start()

    def mask(slot, matrix):
        for p in range(2):
            for q in range(2):
                keep = jnp.full((1, TILE_SIZE), mask_ref[p, q], jnp.int32).astype(F32).astype(BF16)
                rows = slice(p * TILE_SIZE, (p + 1) * TILE_SIZE)
                left = slot * COLS + q * TILE_SIZE
                block = matrix[rows, q * TILE_SIZE : (q + 1) * TILE_SIZE]
                masked[rows, left : left + TILE_SIZE] = block * keep

    for aux in range(AUX):
        mask(aux, own_ref.at[aux])
    for part, copy in enumerate(copies):
        copy.wait()
        for aux in range(SHARE):
            mask(AUX + part * SHARE + aux, factors.at[part, aux])

    zeta = jnp.zeros((2 * AUX, COLS), F32)
    for at_y in range(Y):
        amp = jnp.concatenate([rows_ref[at_x * Y + at_y, :ROWS] for at_x in range(VIRT)], axis=0)
        fac = jnp.concatenate([rows_ref[at_x * Y + at_y, ROWS:] for at_x in range(VIRT)], axis=0)
        direct = lax.dot_general(fac, amp, NT, preferred_element_type=F32)
        swapped = jnp.dot(fac, amp, preferred_element_type=F32)
        zeta = zeta + (2.0 * direct - swapped)
        for slot in range(2 * AUX):
            cols = slice(slot * COLS, (slot + 1) * COLS)
            weighted[:, cols] = jnp.dot(masked[:, cols], amp, preferred_element_type=F32).astype(BF16)
        total = lax.dot_general(weighted[...], masked[...], NT, preferred_element_type=F32).astype(BF16)
        for at_x in range(VIRT):
            out_ref[at_x * Y + at_y, :ROWS] = total[at_x * ROWS : (at_x + 1) * ROWS]
    group = lax.broadcasted_iota(jnp.int32, (PART, COLS), 1) // ROWS
    for at_x in range(VIRT):
        piece = jnp.zeros((PART, COLS), F32)
        for to in range(4):
            turned = zeta[to * PART : (to + 1) * PART]
            if to != at_x:
                turned = pltpu.roll(turned, ((to - at_x) % 4) * ROWS, 1)
            piece = jnp.where(group == to, turned, piece)
        piece = piece.astype(BF16)
        for at_y in range(Y):
            out_ref[at_x * Y + at_y, ROWS:] = piece


def sum_kernel(got_ref, out_ref):
    sums = [jnp.zeros((PART, COLS), F32), jnp.zeros((PART, COLS), F32)]
    for at_x in range(VIRT):
        for low in range(2):
            first = got_ref[at_x * Y + low]
            second = got_ref[at_x * Y + 2 + low]
            out_ref[2 * at_x + low, :ROWS] = (first[:ROWS].astype(F32) + second[:ROWS].astype(F32)).astype(BF16)
            sums[0] = sums[0] + first[ROWS:].astype(F32)
            sums[1] = sums[1] + second[ROWS:].astype(F32)
    group = lax.broadcasted_iota(jnp.int32, (PART, COLS), 1) // ROWS
    halves = []
    for half in range(2):
        piece = jnp.zeros((PART, COLS), F32)
        for high in range(2):
            for low in range(2):
                source, to = 2 * low + half, 2 * high + low
                turned = sums[high]
                if source != to:
                    turned = pltpu.roll(turned, ((to - source) % 4) * ROWS, 1)
                piece = jnp.where(group == to, turned, piece)
        halves.append(piece)
    zeta = jnp.concatenate(halves, axis=0).astype(BF16)
    for to in range(Z):
        out_ref[to, ROWS:] = zeta


def scale_kernel(domain_ref, occ_i_ref, occ_j_ref, virt_ref, out_ref):
    x = lax.axis_index("virt")
    energy = jnp.broadcast_to(virt_ref[...], (ROWS, COLS))
    row = lax.broadcasted_iota(jnp.int32, (ROWS, COLS), 0) + x * ROWS
    lane = lax.broadcasted_iota(jnp.int32, (ROWS, COLS), 1)
    energy_rows = jnp.sum(jnp.where(row == lane, energy, 0.0), axis=1, keepdims=True)
    denom = energy_rows + energy - occ_i_ref[0] - occ_j_ref[0]
    row_tile = domain_ref[0, 0, x // 2]
    left = (row_tile * domain_ref[0, 0, 0]).astype(F32)
    right = (row_tile * domain_ref[0, 0, 1]).astype(F32)
    out_ref[...] = jnp.where(lane < TILE_SIZE, left, right) / denom


def update_kernel(got_ref, ov_ref, scale_ref, out_ref):
    total = got_ref[0, :ROWS].astype(F32)
    for source in range(1, Z):
        total = total + got_ref[source, :ROWS].astype(F32)
    zeta = got_ref[:, ROWS:].reshape(Z * AUX, COLS)
    for at_y in range(Y):
        part = zeta[:, at_y * ROWS : (at_y + 1) * ROWS]
        fac = ov_ref[at_y * Z * AUX : (at_y + 1) * Z * AUX, :]
        total = total + lax.dot_general(part, fac, TN, preferred_element_type=F32)
    out_ref[0, 0] = (total * scale_ref[...]).astype(BF16)


def kernel(function, shape, scalars, arrays, scratch=(), mib=16, dtype=BF16):
    smem = pl.BlockSpec(memory_space=pltpu.SMEM)
    vmem = pl.BlockSpec(memory_space=pltpu.VMEM)
    call = pl.pallas_call(
        function,
        name=function.__name__,
        in_specs=[smem] * len(scalars) + [vmem] * len(arrays),
        out_specs=vmem,
        out_shape=jax.ShapeDtypeStruct(shape, dtype),
        scratch_shapes=list(scratch),
        compiler_params=pltpu.CompilerParams(vmem_limit_bytes=mib << 20),
    )
    return call(*scalars, *arrays)


def body(
    amplitudes,
    vv_factors,
    ov_factors,
    occ_energy_i,
    occ_energy_j,
    virt_energy,
    vv_mask,
    pair_domain,
):
    ov = ov_factors[:, 0, :]
    hbm = pl.BlockSpec(memory_space=pltpu.HBM)
    vmem = pl.BlockSpec(memory_space=pltpu.VMEM)
    share = jax.ShapeDtypeStruct((SHARE, COLS, COLS), BF16)
    sent, up = pl.pallas_call(
        out_kernel,
        name="out_kernel",
        in_specs=[hbm, hbm, hbm, hbm],
        out_specs=[vmem, vmem],
        out_shape=[jax.ShapeDtypeStruct((Z, ROWS + AUX, COLS), BF16), share],
        scratch_shapes=[
            pltpu.SMEM((1, 2), jnp.int32),
            pltpu.VMEM((ROWS, COLS), BF16),
            pltpu.SemaphoreType.DMA((3 + 2 * Z,)),
        ],
    )(pair_domain, amplitudes, ov, vv_factors)
    down = pl.pallas_call(
        down_kernel,
        name="down_kernel",
        in_specs=[hbm],
        out_specs=vmem,
        out_shape=share,
        scratch_shapes=[pltpu.SemaphoreType.DMA],
    )(vv_factors)
    got = lax.all_to_all(sent, "z", 0, 0, tiled=True)
    sent = kernel(spread_kernel, (VIRT * Y, ROWS + PART, COLS), (), (got,))
    swap = [(0, 1), (1, 0)]
    up = lax.ppermute(up, "y", [(y, (y + 1) % Y) for y in range(Y)])
    down = lax.ppermute(down, "y", [(y, (y - 1) % Y) for y in range(Y)])
    extra = (up, down, lax.ppermute(up, "pair", swap), lax.ppermute(down, "pair", swap))
    got = lax.all_to_all(sent, ("virt", "y"), 0, 0, tiled=True)
    wide = pltpu.VMEM((COLS, 2 * AUX * COLS), BF16)
    sent = pl.pallas_call(
        ladder_kernel,
        name="ladder_kernel",
        in_specs=[pl.BlockSpec(memory_space=pltpu.SMEM)] + [pl.BlockSpec(memory_space=pltpu.VMEM)] * 2 + [hbm] * 4,
        out_specs=pl.BlockSpec(memory_space=pltpu.VMEM),
        out_shape=jax.ShapeDtypeStruct((VIRT * Y, ROWS + PART, COLS), BF16),
        scratch_shapes=[
            pltpu.VMEM((4, SHARE, COLS, COLS), BF16),
            wide,
            wide,
            pltpu.SemaphoreType.DMA((4,)),
        ],
        compiler_params=pltpu.CompilerParams(vmem_limit_bytes=40 << 20),
    )(vv_mask, got, vv_factors, *[pltpu.with_memory_space_constraint(part, pltpu.HBM) for part in extra])
    scalars = (pair_domain, occ_energy_i, occ_energy_j)
    scale = kernel(scale_kernel, (ROWS, COLS), scalars, (virt_energy[None, :],), dtype=F32)
    sent, scale = lax.optimization_barrier((sent, scale))
    got = lax.all_to_all(sent, ("virt", "y"), 0, 0, tiled=True)
    sent = kernel(sum_kernel, (Z, ROWS + AUX, COLS), (), (got,))
    got = lax.all_to_all(sent, "z", 0, 0, tiled=True)
    return kernel(update_kernel, (1, 1, ROWS, COLS), (), (got, ov, scale))


def solution(mesh):
    fine = Mesh(mesh.devices.reshape(2, VIRT, Y, Z), ("pair", "virt", "y", "z"))
    integ = ("y", "z")
    placed = (
        P("pair", integ, "virt", None),
        P(integ, None, None),
        P(None, integ, None),
        P("pair"),
        P(integ),
        P(),
        P(),
        P("pair", integ, None),
    )
    return jax.shard_map(
        body,
        mesh=fine,
        in_specs=placed,
        out_specs=P("pair", integ, "virt", None),
        check_vma=False,
    )
```
